128 devices in a mesh: seq: 16 (over z, y), tp: 8 (over x, core).
Axes of the slice: x: 4, y: 4, z: 4, core: 2. Of those that a mesh axis runs over, the one named last changes fastest.
Arguments:
- queries: bfloat16 [4096, 8192], P('seq', 'tp'), may hold values from -6 to 6
- key_matrix: bfloat16 [4096, 1024], P('seq', 'tp'), may hold values from -6 to 6
- value_matrix: bfloat16 [4096, 1024], P('seq', 'tp'), may hold values from -6 to 6
- output_gradient: bfloat16 [4096, 8192], P(('seq', 'tp')), may hold values from -6 to 6
- document: int32 [4096], P('seq'), may hold values from 0 to 7, never falling along the last dimension, each value on 1 to 2048 neighbouring positions
Outputs:
- query_grad: bfloat16 [4096, 8192], P('seq', 'tp')
- key_gradient: bfloat16 [4096, 1024], P('seq', 'tp')
- value_gradient: bfloat16 [4096, 1024], P('seq', 'tp')
The draws below stay inside these ranges and needn't reach their ends.
Inputs may be any that keep to these rules, and one draw needn't show every extreme that they name: document never falls along the sequence; there are exactly 8 documents, each of at most 2048 tokens, and one holds exactly that many.
All inputs are finite; a program needn't handle non-finite values.
Results may differ from the reference program's by a relative error of at most 0.009.
Values may be sent and summed in bfloat16 or wider, within the bound.
A program may use at most 64 MiB of HBM per device.

```python
import math
import jax
import jax.numpy as jnp
import numpy as np
from jax import lax

QUERY_HEADS = 64
KEY_VALUE_HEADS = 8
HEAD_WIDTH = 128
DOCS = 8
WINDOW_TOKENS = 4096


def draw_queries(key, part):
    random_seed_key = jax.random.fold_in(key, 3)
    gaussian_draws = jax.random.normal(random_seed_key, (WINDOW_TOKENS, QUERY_HEADS * HEAD_WIDTH), jnp.float32)
    return jnp.clip(gaussian_draws, -6.0, 6.0).astype(jnp.bfloat16)


def draw_key_matrix(key, part):
    random_seed_key = jax.random.fold_in(key, 5)
    gaussian_draws = jax.random.normal(random_seed_key, (WINDOW_TOKENS, KEY_VALUE_HEADS * HEAD_WIDTH), jnp.float32)
    return jnp.clip(gaussian_draws, -6.0, 6.0).astype(jnp.bfloat16)


def levels(own_key, shape, pieces, least, top_value):
    def one(position, shards_of):
        steps = jax.random.uniform(jax.random.fold_in(jax.random.fold_in(own_key, 6), position), (shards_of,), jnp.float32, least / len(pieces), top_value / len(pieces))
        return jnp.repeat(jnp.exp(steps), shape[position] // shards_of).reshape((-1,) + (1,) * (len(shape) - position - 1))

    loudness = one(*pieces[0])
    for cut in pieces[1:]:
        loudness = loudness * one(*cut)
    return loudness


def length_profile(count, total, bound, slope):
    weights = [(1 << 20) // math.isqrt(grade ** slope) + 1 for grade in range(2, count + 1)]
    surplus, holding = total - bound - (count - 1), [1] * (count - 1)
    while surplus > 0:
        free = [i for i in range(count - 1) if holding[i] < bound]
        whole, left = sum([weights[i] for i in free]), surplus
        for i in free:
            addition = min(bound - holding[i], max(1, left * weights[i] // whole), surplus)
            holding[i] = holding[i] + addition
            surplus = surplus - addition
    return np.array([bound] + holding)


def ragged(own_key, amount, total, bound, slope):
    if amount == 2:
        one = jax.random.randint(own_key, (), max(1, total - bound), min(bound, total - 1) + 1)
        return jnp.stack([one, total - one])
    sizes = jnp.asarray(length_profile(amount, total, bound, slope), jnp.int32)
    twos = (amount - 1) // 2
    donor, sink = sizes[1:1 + 2 * twos:2], sizes[2:2 + 2 * twos:2]
    slack = jnp.minimum(donor - 1, bound - sink)
    shifted = jax.random.randint(jax.random.fold_in(own_key, 1), (twos,), 0, 1 << 20) % (slack + 1)
    sizes = sizes.at[1:1 + 2 * twos:2].set(donor - shifted).at[2:2 + 2 * twos:2].set(sink + shifted)
    return sizes[jax.random.permutation(jax.random.fold_in(own_key, 2), amount)]


def normal_values(key, extent, width, bound, pieces=(), held_as=jnp.bfloat16):
    drawn = width * jax.random.normal(key, extent, jnp.float32)
    if pieces:
        drawn = drawn * levels(key, extent, pieces, -0.22, 0.18)
    return jnp.clip(drawn, -bound, bound).astype(held_as)


def setup_inputs(seed: int = 0) -> dict:
    seeds = jax.random.split(jax.random.key(seed), 6)
    return {
        "queries": draw_queries(jax.random.fold_in(seeds[5], 71), 0),
        "key_matrix": draw_key_matrix(jax.random.fold_in(seeds[5], 71), 0),
        "value_matrix": normal_values(seeds[2], (WINDOW_TOKENS, KEY_VALUE_HEADS * HEAD_WIDTH), 1.0, 6.0, ((0, 16), (1, 8))),
        "output_gradient": normal_values(seeds[3], (WINDOW_TOKENS, QUERY_HEADS * HEAD_WIDTH), 1.0, 6.0, ((0, 128),)),
        "document": jnp.searchsorted(jnp.cumsum(ragged(seeds[4], DOCS, WINDOW_TOKENS, WINDOW_TOKENS // 2, 2)), jnp.arange(WINDOW_TOKENS), side="right").astype(jnp.int32),
    }


neg_big = -1e+30

def reference(queries, key_matrix, value_matrix, output_gradient, document):
    group_width = QUERY_HEADS // KEY_VALUE_HEADS
    factor = 1.0 / math.sqrt(HEAD_WIDTH)
    query_head_rows = jnp.transpose(queries.reshape(WINDOW_TOKENS, KEY_VALUE_HEADS, group_width, HEAD_WIDTH), (1, 0, 2, 3))
    gradient_heads = jnp.transpose(output_gradient.reshape(WINDOW_TOKENS, KEY_VALUE_HEADS, group_width, HEAD_WIDTH), (1, 0, 2, 3))
    key_head_rows = jnp.transpose(key_matrix.reshape(WINDOW_TOKENS, KEY_VALUE_HEADS, HEAD_WIDTH), (1, 0, 2))
    value_head_rows = jnp.transpose(value_matrix.reshape(WINDOW_TOKENS, KEY_VALUE_HEADS, HEAD_WIDTH), (1, 0, 2))
    rows_blk = math.gcd(WINDOW_TOKENS, 512)
    positions = jnp.arange(WINDOW_TOKENS, dtype=jnp.int32)

    def one_head(operands):
        query_one, grad_one, key_one, value_one = operands
        key_f = key_one.astype(jnp.float32)
        value_f = value_one.astype(jnp.float32)

        def query_block(carry, block_index):
            key_acc, value_acc = carry
            start_row = (block_index * rows_blk).astype(jnp.int32)
            query_blk = lax.dynamic_slice_in_dim(query_one, start_row, rows_blk, 0).astype(jnp.float32)
            grad_blk = lax.dynamic_slice_in_dim(grad_one, start_row, rows_blk, 0).astype(jnp.float32)
            doc_blk = lax.dynamic_slice_in_dim(document, start_row, rows_blk, 0)
            pos_blk = start_row + jnp.arange(rows_blk, dtype=jnp.int32)
            visible = (doc_blk[:, None] == document[None, :]) & (positions[None, :] <= pos_blk[:, None])
            scores = jnp.einsum('igd,jd->gij', query_blk, key_f) * factor
            scores = jnp.where(visible[None], scores, neg_big)
            row_peak = lax.optimization_barrier(jnp.max(scores, axis=-1))
            row_total = lax.optimization_barrier(jnp.sum(jnp.where(visible[None], jnp.exp(scores - row_peak[..., None]), 0.0), axis=-1))
            log_total = row_peak + jnp.log(row_total)
            weights = jnp.where(visible[None], jnp.exp(scores - log_total[..., None]), 0.0)
            weight_grad = jnp.einsum('igd,jd->gij', grad_blk, value_f)
            row_dot = lax.optimization_barrier(jnp.sum(weights * weight_grad, axis=-1))
            weights_half = lax.optimization_barrier(weights.astype(jnp.bfloat16)).astype(jnp.float32)
            score_grad = lax.optimization_barrier((weights * (weight_grad - row_dot[..., None])).astype(jnp.bfloat16)).astype(jnp.float32)
            value_acc = value_acc + jnp.einsum('gij,igd->jd', weights_half, grad_blk)
            key_acc = key_acc + jnp.einsum('gij,igd->jd', score_grad, query_blk)
            query_part = jnp.einsum('gij,jd->igd', score_grad, key_f)
            return ((key_acc, value_acc), query_part)
        zero_keys = jnp.zeros((WINDOW_TOKENS, HEAD_WIDTH), jnp.float32)
        (key_acc, value_acc), query_parts = lax.scan(query_block, (zero_keys, zero_keys), jnp.arange(WINDOW_TOKENS // rows_blk, dtype=jnp.int32))
        query_grad = query_parts.reshape(WINDOW_TOKENS, group_width, HEAD_WIDTH) * factor
        return (query_grad, key_acc * factor, value_acc)
    query_all, key_full, value_full = lax.map(one_head, (query_head_rows, gradient_heads, key_head_rows, value_head_rows))
    query_grad = jnp.transpose(query_all, (1, 0, 2, 3)).reshape(WINDOW_TOKENS, QUERY_HEADS * HEAD_WIDTH).astype(jnp.bfloat16)
    key_gradient = jnp.transpose(key_full, (1, 0, 2)).reshape(WINDOW_TOKENS, KEY_VALUE_HEADS * HEAD_WIDTH).astype(jnp.bfloat16)
    value_gradient = jnp.transpose(value_full, (1, 0, 2)).reshape(WINDOW_TOKENS, KEY_VALUE_HEADS * HEAD_WIDTH).astype(jnp.bfloat16)
    return (query_grad, key_gradient, value_gradient)
```

```python
import functools
import math

import jax
import jax.numpy as jnp
from jax import lax
from jax.experimental import pallas as pl
from jax.experimental.pallas import tpu as pltpu
from jax.sharding import PartitionSpec as P

MESH = pl.DeviceIdType.MESH
F32 = jnp.float32
BF16 = jnp.bfloat16
HEAD = 128
FACTOR = 1.0 / math.sqrt(HEAD)
FACTOR2 = FACTOR * math.log2(math.e)
BIG = -1e30
PAD = 16


def dot_nt(a, b):
    return lax.dot_general(a, b, (((1,), (1,)), ((), ())), preferred_element_type=F32)


def dot_nn(a, b):
    return lax.dot_general(a, b, (((1,), (0,)), ((), ())), preferred_element_type=F32)


def kernel(
    n_seq, n_tp, back,
    q, k, v, do, doc,
    dq, dk, dv,
    kv, dog, scores, wgrad, keysT, kacc, vacc, part, got,
    kv_send, kv_recv, do_send, do_recv, rs_send, rs_recv,
):
    s = lax.axis_index("seq")
    t = lax.axis_index("tp")
    tokens = q.shape[0]
    heads = q.shape[1] // HEAD
    rows_do = do.shape[0]
    cols = q.shape[1]

    barrier = pltpu.get_barrier_semaphore()
    for d in range(1, n_tp):
        pl.semaphore_signal(
            barrier, inc=1, device_id={"tp": lax.rem(t + d, n_tp)}, device_id_type=MESH
        )
    for d in range(1, n_seq):
        pl.semaphore_signal(
            barrier, inc=1, device_id={"seq": lax.rem(s + d, n_seq)}, device_id_type=MESH
        )

    kv[back, 0:tokens, 0:HEAD] = k[...]
    kv[back, 0:tokens, HEAD : 2 * HEAD] = v[...]
    kv[back, tokens : tokens + PAD, :] = jnp.broadcast_to(doc[...].astype(F32), (PAD, tokens)).astype(BF16)
    for d in range(1, back + 1):

        @pl.when(s < d)
        def _():
            kv[back - d, 0:tokens, :] = jnp.zeros((tokens, 2 * HEAD), BF16)
            kv[back - d, tokens : tokens + PAD, :] = jnp.full((PAD, tokens), -1.0, BF16)

    dog[pl.ds(pl.multiple_of(t * rows_do, rows_do), rows_do), :] = do[
        :, pl.ds(pl.multiple_of(t * cols, cols), cols)
    ]
    pl.semaphore_wait(barrier, n_tp - 1 + n_seq - 1)

    do_copies = []
    for d in range(1, n_tp):
        p = lax.rem(t + d, n_tp)
        c = pltpu.make_async_remote_copy(
            do.at[:, pl.ds(pl.multiple_of(p * cols, cols), cols)],
            dog.at[pl.ds(pl.multiple_of(t * rows_do, rows_do), rows_do), :],
            do_send.at[d - 1],
            do_recv.at[d - 1],
            device_id={"tp": p},
            device_id_type=MESH,
        )
        c.start()
        do_copies.append(c)

    def kv_copy(d):
        return pltpu.make_async_remote_copy(
            kv.at[back],
            kv.at[back - d],
            kv_send.at[d - 1],
            kv_recv.at[d - 1],
            device_id={"seq": lax.rem(s + d, n_seq)},
            device_id_type=MESH,
        )

    for d in range(1, back + 1):

        @pl.when(s + d < n_seq)
        def _():
            kv_copy(d).start()

    for d in range(1, back + 1):

        @pl.when(s >= d)
        def _():
            kv_copy(d).wait_recv()

    for c in do_copies:
        c.wait_recv()

    own_doc = doc[...].astype(F32)
    start = jnp.zeros((1, tokens), F32)
    docs = [kv[b, tokens : tokens + 1, :].astype(F32) for b in range(back + 1)]
    for d in range(8):
        hits = sum(jnp.where(x < d, 1.0, 0.0) for x in docs)
        count = jnp.sum(hits, axis=1, keepdims=True)
        start = start + jnp.where(own_doc == d, count, 0.0)
    start = start.astype(jnp.int32)

    for b in range(back + 1):
        keysT[:, b * tokens : (b + 1) * tokens] = kv[b, 0:tokens, 0:HEAD].astype(F32).T.astype(BF16)
    kacc[...] = jnp.zeros_like(kacc)
    vacc[...] = jnp.zeros_like(vacc)
    key_at = lax.broadcasted_iota(jnp.int32, (tokens, tokens), 0)
    query_at = lax.broadcasted_iota(jnp.int32, (tokens, tokens), 1)

    def one_head(h, carry):
        hs = pl.ds(pl.multiple_of(h * HEAD, HEAD), HEAD)
        qh = q[:, hs]
        gh = dog[:, hs]
        peak = jnp.full((1, tokens), BIG, F32)
        for b in range(back + 1):
            r = slice(b * tokens, (b + 1) * tokens)
            sc = dot_nt(kv[b, 0:tokens, 0:HEAD], qh)
            seen = key_at >= start - b * tokens
            if b == back:
                seen = seen & (key_at <= query_at)
            sc = jnp.where(seen, sc, BIG)
            peak = jnp.maximum(peak, jnp.max(sc, axis=0, keepdims=True))
            scores[r, :] = sc
            wgrad[r, :] = dot_nt(kv[b, 0:tokens, HEAD : 2 * HEAD], gh)
        total = jnp.zeros((1, tokens), F32)
        weighted = jnp.zeros((1, tokens), F32)
        for b in range(back + 1):
            r = slice(b * tokens, (b + 1) * tokens)
            e = jnp.exp2((scores[r, :] - peak) * FACTOR2)
            total = total + jnp.sum(e, axis=0, keepdims=True)
            weighted = weighted + jnp.sum(e * wgrad[r, :], axis=0, keepdims=True)
            scores[r, :] = e
        inv = 1.0 / total
        row_dot = weighted * inv
        dq_t = jnp.zeros((HEAD, tokens), F32)
        for b in range(back + 1):
            r = slice(b * tokens, (b + 1) * tokens)
            p = scores[r, :] * inv
            ds = (p * (wgrad[r, :] - row_dot)).astype(BF16)
            vacc[r, :] += dot_nn(p.astype(BF16), gh)
            kacc[r, :] += dot_nn(ds, qh)
            dq_t = dq_t + dot_nn(keysT[:, r], ds)
        dq[:, hs] = (dq_t.T * FACTOR).astype(BF16)
        return carry

    lax.fori_loop(0, heads, one_head, 0)

    def rs_copy(d):
        return pltpu.make_async_remote_copy(
            part.at[d - 1],
            got.at[d - 1],
            rs_send.at[d - 1],
            rs_recv.at[d - 1],
            device_id={"seq": lax.rem(s - d + n_seq, n_seq)},
            device_id_type=MESH,
        )

    for d in range(1, back + 1):
        r = slice((back - d) * tokens, (back - d + 1) * tokens)
        part[d - 1, :, 0:HEAD] = (kacc[r, :] * FACTOR).astype(BF16)
        part[d - 1, :, HEAD : 2 * HEAD] = vacc[r, :].astype(BF16)

    for d in range(1, back + 1):

        @pl.when(s >= d)
        def _():
            rs_copy(d).start()

    r = slice(back * tokens, (back + 1) * tokens)
    kacc[r, :] = kacc[r, :] * FACTOR
    for d in range(1, back + 1):

        @pl.when(s + d < n_seq)
        def _():
            rs_copy(d).wait_recv()
            kacc[r, :] += got[d - 1, :, 0:HEAD].astype(F32)
            vacc[r, :] += got[d - 1, :, HEAD : 2 * HEAD].astype(F32)

    dk[...] = kacc[r, :].astype(BF16)
    dv[...] = vacc[r, :].astype(BF16)

    for c in do_copies:
        c.wait_send()
    for d in range(1, back + 1):

        @pl.when(s + d < n_seq)
        def _():
            kv_copy(d).wait_send()

        @pl.when(s >= d)
        def _():
            rs_copy(d).wait_send()


def solution(mesh):
    n_seq, n_tp = mesh.shape["seq"], mesh.shape["tp"]

    def local(queries, key_matrix, value_matrix, output_gradient, document):
        tokens, cols = queries.shape
        back = 8
        width = (back + 1) * tokens
        vm = pl.BlockSpec(memory_space=pltpu.VMEM)
        dma = pltpu.SemaphoreType.DMA
        return pl.pallas_call(
            functools.partial(kernel, n_seq, n_tp, back),
            out_shape=[
                jax.ShapeDtypeStruct((tokens, cols), BF16),
                jax.ShapeDtypeStruct((tokens, HEAD), BF16),
                jax.ShapeDtypeStruct((tokens, HEAD), BF16),
            ],
            in_specs=[vm] * 5,
            out_specs=[vm] * 3,
            scratch_shapes=[
                pltpu.VMEM((back + 1, tokens + PAD, 2 * HEAD), BF16),
                pltpu.VMEM((tokens, cols), BF16),
                pltpu.VMEM((width, tokens), F32),
                pltpu.VMEM((width, tokens), F32),
                pltpu.VMEM((HEAD, width), BF16),
                pltpu.VMEM((width, HEAD), F32),
                pltpu.VMEM((width, HEAD), F32),
                pltpu.VMEM((back, tokens, 2 * HEAD), BF16),
                pltpu.VMEM((back, tokens, 2 * HEAD), BF16),
                dma((back,)), dma((back,)), dma((n_tp - 1,)), dma((n_tp - 1,)), dma((back,)), dma((back,)),
            ],
            compiler_params=pltpu.CompilerParams(
                collective_id=0, has_side_effects=True, vmem_limit_bytes=48 * 1024 * 1024
            ),
        )(queries, key_matrix, value_matrix, output_gradient, document.reshape(1, tokens))

    return jax.shard_map(
        local,
        mesh=mesh,
        in_specs=(P("seq", "tp"), P("seq", "tp"), P("seq", "tp"), P(("seq", "tp"), None), P("seq")),
        out_specs=(P("seq", "tp"),) * 3,
        check_vma=False,
    )
```

```python
import functools
import math

import jax
import jax.numpy as jnp
from jax import lax
from jax.experimental import pallas as pl
from jax.experimental.pallas import tpu as pltpu
from jax.sharding import PartitionSpec as P

MESH = pl.DeviceIdType.MESH
F32 = jnp.float32
BF16 = jnp.bfloat16
HEAD = 128
ROW = 4
DOCS = 8
FACTOR = 1.0 / math.sqrt(HEAD)
FACTOR2 = FACTOR * math.log2(math.e)
BIG = -1e30
PAD = 16


def dot_nt(a, b):
    return lax.dot_general(a, b, (((1,), (1,)), ((), ())), preferred_element_type=F32)


def dot_nn(a, b):
    return lax.dot_general(a, b, (((1,), (0,)), ((), ())), preferred_element_type=F32)


def pick(index, values):
    out = values[-1]
    for i in range(len(values) - 2, -1, -1):
        out = jnp.where(index == i, values[i], out)
    return out


def kernel(
    n_seq, n_tp,
    q_in, k_in, v_in, do_in, doc,
    dq_out, dk_out, dv_out,
    q, do, dog, kbuf, vbuf, qs, gs, keysT,
    e_ref, p_ref, ds_ref, pb_ref, peak_blk, w_blk, f_ref, peak, total, row_dot,
    pk, pv, rel, msg_a, msg_b, down, out_qt, dq_v, dkv,
    in_sem, out_sem, do_send, do_recv, kv_send, kv_recv, rs_send, rs_recv,
):
    s = lax.axis_index("seq")
    t = lax.axis_index("tp")
    z = s // ROW
    y = lax.rem(s, ROW)
    rows = n_seq // ROW
    tokens, cols = q.shape
    heads = cols // HEAD
    rows_do = do.shape[0]
    right = {"seq": z * ROW + lax.rem(y + 1, ROW)}
    left = {"seq": z * ROW + lax.rem(y + ROW - 1, ROW)}

    barrier = pltpu.get_barrier_semaphore()
    for d in range(1, n_tp):
        pl.semaphore_signal(barrier, inc=1, device_id={"tp": lax.rem(t + d, n_tp)}, device_id_type=MESH)
    near = [z * ROW + lax.rem(y + d, ROW) for d in (1, 3)]
    near += [lax.rem(z + d, rows) * ROW + y for d in (1, 2, 3)]
    for n in near:
        pl.semaphore_signal(barrier, inc=1, device_id={"seq": n}, device_id_type=MESH)

    own = 8 + y
    loads = [
        pltpu.make_async_copy(k_in, kbuf.at[own, 0:tokens], in_sem.at[0]),
        pltpu.make_async_copy(v_in, vbuf.at[own], in_sem.at[1]),
        pltpu.make_async_copy(q_in, q, in_sem.at[2]),
        pltpu.make_async_copy(do_in, do, in_sem.at[3]),
    ]
    for c in loads:
        c.start()
    docf = doc[...].astype(F32)
    kbuf[own, tokens : tokens + PAD, :] = jnp.concatenate(
        [docf[:, 0:HEAD], docf[:, HEAD:], jnp.zeros((PAD - 2, HEAD), F32)], axis=0
    ).astype(BF16)
    for r in range(2):

        @pl.when(z + r < 2)
        def _():
            for i in range(ROW):
                kbuf[r * ROW + i, 0:tokens, :] = jnp.zeros((tokens, HEAD), BF16)
                kbuf[r * ROW + i, tokens : tokens + PAD, :] = jnp.full((PAD, HEAD), -1.0, BF16)
                vbuf[r * ROW + i, :, :] = jnp.zeros((tokens, HEAD), BF16)

    for c in loads:
        c.wait()
    pl.semaphore_wait(barrier, n_tp - 1 + len(near))

    started = []

    def send(when, src, dst, ssem, rsem, to):
        def make():
            return pltpu.make_async_remote_copy(src(), dst(), ssem(), rsem(), device_id=to, device_id_type=MESH)

        @pl.when(when())
        def _():
            make().start()

        started.append((when, make))

    def send_block(when, slot, dst_slot, half, index, to):
        buf = (kbuf, vbuf)[half]
        send(
            when, lambda: buf.at[slot], lambda: buf.at[dst_slot],
            lambda: kv_send.at[index], lambda: kv_recv.at[2 * dst_slot + half], to,
        )

    def wait_block(when, slot, halves=(0, 1)):
        for half in halves:
            buf = (kbuf, vbuf)[half]

            @pl.when(when)
            def _():
                pltpu.make_async_remote_copy(
                    buf.at[slot], buf.at[slot], kv_send.at[0], kv_recv.at[2 * slot + half],
                    device_id=right, device_id_type=MESH,
                ).wait_recv()

    has1, has2 = z >= 1, z >= 2
    for half in range(2):
        send_block(lambda: z + 1 < rows, own, 4 + y, half, half, {"seq": lax.rem(s + ROW, n_seq)})
    for half in range(2):
        send_block(lambda: y <= 2, own, own, half, 2 + half, right)
        send_block(lambda: y == 0, own, own, half, 4 + half, left)
    for half in range(2):
        send_block(lambda: z + 2 < rows, own, y, half, 6 + half, {"seq": lax.rem(s + 2 * ROW, n_seq)})
    do_copies = []
    for d in (2, 6, 4, 3, 5, 7, 1):
        p = lax.rem(t + d, n_tp)
        c = pltpu.make_async_remote_copy(
            do.at[:, pl.ds(pl.multiple_of(p * cols, cols), cols)],
            dog.at[pl.ds(pl.multiple_of(t * rows_do, rows_do), rows_do), :],
            do_send.at[d - 1],
            do_recv.at[d - 1],
            device_id={"tp": p},
            device_id_type=MESH,
        )
        c.start()
        do_copies.append(c)
    dog[pl.ds(pl.multiple_of(t * rows_do, rows_do), rows_do), :] = do[
        :, pl.ds(pl.multiple_of(t * cols, cols), cols)
    ]

    col1, own_left, y1, y2 = 4 + y, own - 1, y + 1, y + 2
    slots_a = [jnp.where(y + e < ROW, y + e, y + e + 4) for e in range(4)]
    slots_b = [4 + lax.rem(y + e, ROW) for e in range(4)]
    to1 = {"seq": lax.rem(s + n_seq - ROW, n_seq)}
    to2 = {"seq": lax.rem(s + n_seq - 2 * ROW, n_seq)}

    def slot_a(e):
        return slots_a[e]

    def slot_b(e):
        return slots_b[e]

    key_at = lax.broadcasted_iota(jnp.int32, (tokens, tokens), 0)
    query_at = lax.broadcasted_iota(jnp.int32, (tokens, tokens), 1)

    def head_rows(h):
        return pl.ds(pl.multiple_of(h * tokens, tokens), tokens)

    for h in range(heads):
        qs[h * tokens : (h + 1) * tokens, :] = q[:, h * HEAD : (h + 1) * HEAD]

    def scores(slot, diagonal):
        w = slot - y
        kb = kbuf[slot, 0:tokens, :]
        docs = kbuf[slot, tokens : tokens + PAD, :].astype(F32)[0:2, :]
        low = jnp.zeros((1, tokens), F32)
        for d in range(DOCS):
            count = jnp.sum(jnp.where(docs < d, 1.0, 0.0), axis=(0, 1), keepdims=True)
            low = low + jnp.where(docf == d, count, 0.0)
        seen = key_at >= low.astype(jnp.int32)
        if diagonal:
            seen = seen & (key_at <= query_at)

        def one(h, c):
            sc = jnp.where(seen, dot_nt(kb, qs[head_rows(h), :]), BIG)
            top = jnp.max(sc, axis=0, keepdims=True)
            if not diagonal:
                old = peak[h]
                top = jnp.maximum(old, top)
            e = jnp.exp2((sc - top) * FACTOR2)
            part = jnp.sum(e, axis=0, keepdims=True)
            if not diagonal:
                part = part + total[h] * jnp.exp2((old - top) * FACTOR2)
            total[h] = part
            peak[h] = top
            peak_blk[w, h] = top
            e_ref[w, h] = e
            return c

        lax.fori_loop(0, heads, one, 0, unroll=2)

    def weight_grads(slot):
        w = slot - y
        vb = vbuf[slot]

        def one(h, c):
            dp = dot_nt(vb, gs[head_rows(h), :])
            p_ref[w, h] = dp
            w_blk[w, h] = jnp.sum(e_ref[w, h] * dp, axis=0, keepdims=True)
            return c

        lax.fori_loop(0, heads, one, 0, unroll=2)

    scores(own, True)

    def first_stage():
        wait_block(has1, 4 + y)
        for half in range(2):
            send_block(lambda: has1, col1, col1, half, 8 + half, right)
            send_block(lambda: has1, col1, col1, half, 10 + half, left)
        wait_block(y >= 1, own - 1)
        wait_block(y == 3, 8)
        send_block(lambda: (y == 1) | (y == 2), own_left, own_left, 0, 12, right)
        send_block(lambda: y == 2, own_left, own_left, 1, 13, right)
        send_block(lambda: y == 3, 8, 8, 1, 14, left)

    def step_slot(k):
        late = k - 6 - y
        return pick(
            k,
            [
                own,
                4 + y,
                *[
                    jnp.where(
                        k < 2 + y,
                        pick(y, [8, 8, jnp.where(k == 2, 9, 8), jnp.where(k == 2, 10, jnp.where(k == 3, 8, 9))]),
                        jnp.where(
                            k < 6 + y,
                            pick(k - 2 - y, [y, slot_b(3), slot_b(1), slot_b(2)]),
                            pick(y, [pick(late, [1, 3, 2]), pick(late, [2, 3]), 3, 3]),
                        ),
                    )
                ]
                * 7,
            ],
        )

    first_stage()

    def gather_do():
        for c in do_copies:
            c.wait_recv()
        for h in range(heads):
            gs[h * tokens : (h + 1) * tokens, :] = dog[:, h * HEAD : (h + 1) * HEAD]

    def loop(k, c):
        @pl.when(k == 2)
        def _():
            wait_block(y == 2, 8)
            wait_block(y == 3, 9)

        @pl.when(k == 2 + y)
        def _():
            wait_block(has2, y)
            for half in range(2):
                send_block(lambda: has2 & (y == 3), y, y, half, 15 + half, right)
                send_block(lambda: has2 & (y >= 1), y, y, half, 17 + half, left)

        @pl.when(k == 3 + y)
        def _():
            wait_block(has1, slot_b(3))
            wait_block(has1, slot_b(1))
            send_block(lambda: has1, slot_b(3), slot_b(3), 0, 19, right)
            send_block(lambda: has1, slot_b(1), slot_b(1), 1, 20, left)

        @pl.when(k == 5 + y)
        def _():
            wait_block(has2 & (y <= 2), y + 1)
            wait_block(has2 & (y == 0), 3)
            send_block(lambda: has2 & (y == 0), 3, 3, 0, 21, right)
            send_block(lambda: has2 & ((y == 1) | (y == 2)), y1, y1, 1, 22, left)
            send_block(lambda: has2 & (y == 1), y1, y1, 0, 23, left)
            wait_block(has1, slot_b(2))

        @pl.when(k == 8)
        def _():
            wait_block(has2 & (y < 2), y + 2)

        @pl.when(k == 6)
        def _():
            gather_do()

            def early(j, c):
                weight_grads(step_slot(j))
                return c

            lax.fori_loop(0, 6, early, 0)

        scores(step_slot(k), False)
        return c

    lax.fori_loop(1, 9, loop, 0)

    def rest(j, c):
        weight_grads(step_slot(j))
        return c

    lax.fori_loop(6, 9, rest, 0)

    def stats(h, c):
        inv = 1.0 / total[h]
        acc = jnp.zeros((1, tokens), F32)
        for w in range(9):
            f = jnp.exp2((peak_blk[w, h] - peak[h]) * FACTOR2) * inv
            f_ref[w, h] = f
            acc = acc + f * w_blk[w, h]
        row_dot[h] = acc
        return c

    lax.fori_loop(0, heads, stats, 0)

    order = [slot_b(2), slot_a(2), slot_b(1), slot_b(3), slot_a(1), slot_a(3), y, 4 + y, own]
    halves = (pk, pv)

    def rs(when, src, dst, index, to):
        send(when, src, dst, lambda: rs_send.at[index], lambda: rs_recv.at[index], to)

    def rs_wait(when, dst, index):
        @pl.when(when)
        def _():
            pltpu.make_async_remote_copy(
                dst, dst, rs_send.at[index], rs_recv.at[index], device_id=right, device_id_type=MESH
            ).wait_recv()

    def add(when, half, slot, other):
        @pl.when(when)
        def _():
            halves[half][slot] = (halves[half][slot].astype(F32) + other[...].astype(F32)).astype(BF16)

    a2_any = has2 | (y >= 2)
    a1_any = has2 | (y == 3)
    a3_any = has2 | (y >= 1)

    def after(j):
        if j == 0:
            rs(lambda: has1, lambda: pk.at[slot_b(2)], lambda: rel.at[0], 0, right)
            rs(lambda: has1, lambda: pv.at[slot_b(2)], lambda: rel.at[1], 1, left)
        if j == 1:
            sl = slot_a(2)
            rs(lambda: has2 & (y == 0), lambda: pk.at[sl], lambda: rel.at[2], 2, right)
            rs(lambda: a2_any & (y >= 1), lambda: pk.at[sl], lambda: rel.at[3], 3, left)
            rs(lambda: a2_any & (y <= 2), lambda: pv.at[sl], lambda: rel.at[4], 4, right)
            rs(lambda: y == 3, lambda: pv.at[sl], lambda: rel.at[5], 5, left)
        if j == 2:
            rs(lambda: has1, lambda: pv.at[slot_b(1)], lambda: msg_b.at[1], 7, right)
        if j == 3:
            rs(lambda: has1, lambda: pk.at[slot_b(3)], lambda: msg_b.at[2], 8, left)
            rs_wait(has1, rel.at[0], 0)
            add(has1, 0, slot_b(1), rel.at[0])
            rs(lambda: has1, lambda: pk.at[slot_b(1)], lambda: msg_b.at[0], 6, right)
            rs_wait(has1, rel.at[1], 1)
            add(has1, 1, slot_b(3), rel.at[1])
            rs(lambda: has1, lambda: pv.at[slot_b(3)], lambda: msg_b.at[3], 9, left)
        if j == 4:
            sl = slot_a(1)
            rs_wait(has2 & (y == 1), rel.at[2], 2)
            add(has2 & (y == 1), 0, sl, rel.at[2])
            rs(lambda: a1_any, lambda: pk.at[sl], lambda: msg_a.at[0], 10, right)
            got_v = (has2 & (y >= 1)) | (y == 3)
            rs_wait(got_v, rel.at[4], 4)
            add(got_v, 1, sl, rel.at[4])
            rs(lambda: a1_any, lambda: pv.at[sl], lambda: msg_a.at[1], 11, right)
        if j == 5:
            sl = slot_a(3)
            got_k = (has2 & (y == 0)) | (y == 1) | (y == 2)
            rs_wait(got_k, rel.at[3], 3)
            add(got_k, 0, sl, rel.at[3])
            rs(lambda: a3_any, lambda: pk.at[sl], lambda: msg_a.at[2], 12, left)
            rs_wait(y == 2, rel.at[5], 5)
            add(y == 2, 1, sl, rel.at[5])
            rs(lambda: a3_any, lambda: pv.at[sl], lambda: msg_a.at[3], 13, left)
        if j == 7:
            for half in range(2):
                rs_wait(has1, msg_b.at[half], 6 + half)
                add(has1, half, 4 + y, msg_b.at[half])
                rs_wait(has1, msg_b.at[2 + half], 8 + half)
                add(has1, half, 4 + y, msg_b.at[2 + half])
                rs(lambda: has1, lambda half=half: halves[half].at[col1], lambda half=half: down.at[half], 14 + half, to1)
            from_left = (has2 & (y >= 1)) | (y == 0)
            from_right = (has2 & (y == 3)) | (y <= 2)
            for half in range(2):
                rs_wait(from_left, msg_a.at[half], 10 + half)
                rs_wait(from_right, msg_a.at[2 + half], 12 + half)
                add(has2 & (y >= 1), half, y, msg_a.at[half])
                add(has2 & (y == 3), half, y, msg_a.at[2 + half])
                rs(lambda: has2, lambda half=half: halves[half].at[y], lambda half=half: down.at[2 + half], 16 + half, to2)

    def matmuls(j):
        slot = pick(j, order)
        buf = lax.rem(j, 2)
        w = slot - y
        dvb = dot_nn(pb_ref[buf], gs[...])
        dkb = dot_nn(ds_ref[w], qs[...]) * FACTOR

        pk[slot] = dkb.astype(BF16)
        pv[slot] = dvb.astype(BF16)

        @pl.when(j == 8)
        def _():
            dkv[0] = dkb
            dkv[1] = dvb

    def elementwise(j):
        slot = pick(j, order)
        buf = lax.rem(j, 2)
        w = slot - y
        for h in range(heads):
            p = e_ref[w, h] * f_ref[w, h]
            ds_ref[w, :, h * tokens : (h + 1) * tokens] = (p * (p_ref[w, h] - row_dot[h])).astype(BF16)
            pb_ref[buf, :, h * tokens : (h + 1) * tokens] = p.astype(BF16)

    elementwise(0)

    def grads(j, c):
        elementwise(j)
        matmuls(j - 1)
        for i in range(8):

            @pl.when(j == i + 1)
            def _():
                after(i)

        return c

    lax.fori_loop(1, 9, grads, 0)
    matmuls(jnp.int32(8))

    for w in range(9):
        keysT[:, w * tokens : (w + 1) * tokens] = kbuf[y + w, 0:tokens, :].astype(F32).T.astype(BF16)

    def query(h, c):
        hs = pl.ds(pl.multiple_of(h * tokens, tokens), tokens)
        acc = jnp.zeros((HEAD, tokens), F32)
        for w in range(9):
            acc = acc + dot_nn(keysT[:, w * tokens : (w + 1) * tokens], ds_ref[w, :, hs])
        dq_v[:, pl.ds(pl.multiple_of(h * HEAD, HEAD), HEAD)] = (acc.T * FACTOR).astype(BF16)
        return c

    lax.fori_loop(0, heads, query, 0)
    dq_copy = pltpu.make_async_copy(dq_v, dq_out, out_sem.at[0])
    dq_copy.start()

    for half in range(2):

        @pl.when(y == 0)
        def _():
            dkv[half] += msg_a[half].astype(F32)

        @pl.when(y <= 2)
        def _():
            dkv[half] += msg_a[2 + half].astype(F32)

    for i, when in ((0, z + 1 < rows), (2, z + 2 < rows)):
        for half in range(2):
            rs_wait(when, down.at[i + half], 14 + i + half)

            @pl.when(when)
            def _():
                dkv[half] += down[i + half].astype(F32)

    down[0] = dkv[0].astype(BF16)
    down[1] = dkv[1].astype(BF16)
    outs = [
        pltpu.make_async_copy(down.at[0], dk_out, out_sem.at[1]),
        pltpu.make_async_copy(down.at[1], dv_out, out_sem.at[2]),
    ]
    for c in outs:
        c.start()
    for c in do_copies:
        c.wait_send()
    for when, make in started:

        @pl.when(when())
        def _():
            make().wait_send()

    for c in outs:
        c.wait()
    dq_copy.wait()


def solution(mesh):
    n_seq, n_tp = mesh.shape["seq"], mesh.shape["tp"]

    def local(queries, key_matrix, value_matrix, output_gradient, document):
        tokens, cols = queries.shape
        heads = cols // HEAD
        hbm = pl.BlockSpec(memory_space=pltpu.HBM)
        vm = pl.BlockSpec(memory_space=pltpu.VMEM)
        dma = pltpu.SemaphoreType.DMA
        v = pltpu.VMEM
        return pl.pallas_call(
            functools.partial(kernel, n_seq, n_tp),
            out_shape=[
                jax.ShapeDtypeStruct((tokens, cols), BF16),
                jax.ShapeDtypeStruct((tokens, HEAD), BF16),
                jax.ShapeDtypeStruct((tokens, HEAD), BF16),
            ],
            in_specs=[hbm] * 4 + [vm],
            out_specs=[hbm] * 3,
            scratch_shapes=[
                v((tokens, cols), BF16),
                v(output_gradient.shape, BF16),
                v((tokens, cols), BF16),
                v((12, tokens + PAD, HEAD), BF16),
                v((12, tokens, HEAD), BF16),
                v((heads * tokens, HEAD), BF16),
                v((heads * tokens, HEAD), BF16),
                v((HEAD, 9 * tokens), BF16),
                v((9, heads, tokens, tokens), F32),
                v((9, heads, tokens, tokens), F32),
                v((9, tokens, heads * tokens), BF16),
                v((2, tokens, heads * tokens), BF16),
                v((9, heads, 1, tokens), F32),
                v((9, heads, 1, tokens), F32),
                v((9, heads, 1, tokens), F32),
                v((heads, 1, tokens), F32),
                v((heads, 1, tokens), F32),
                v((heads, 1, tokens), F32),
                v((12, tokens, HEAD), BF16),
                v((12, tokens, HEAD), BF16),
                v((6, tokens, HEAD), BF16),
                v((4, tokens, HEAD), BF16),
                v((4, tokens, HEAD), BF16),
                v((4, tokens, HEAD), BF16),
                v((8, HEAD), F32),
                v((tokens, cols), BF16),
                v((2, tokens, HEAD), F32),
                dma((4,)), dma((3,)), dma((n_tp - 1,)), dma((n_tp - 1,)),
                dma((24,)), dma((24,)), dma((18,)), dma((18,)),
            ],
            compiler_params=pltpu.CompilerParams(
                collective_id=0, has_side_effects=True, vmem_limit_bytes=63 * 1024 * 1024
            ),
        )(queries, key_matrix, value_matrix, output_gradient, document.reshape(1, tokens))

    return jax.shard_map(
        local,
        mesh=mesh,
        in_specs=(P("seq", "tp"), P("seq", "tp"), P("seq", "tp"), P(("seq", "tp"), None), P("seq")),
        out_specs=(P("seq", "tp"),) * 3,
        check_vma=False,
    )
```

```python
import functools
import math

import jax
import jax.numpy as jnp
from jax import lax
from jax.experimental import pallas as pl
from jax.experimental.pallas import tpu as pltpu
from jax.sharding import PartitionSpec as P

MESH = pl.DeviceIdType.MESH
F32 = jnp.float32
BF16 = jnp.bfloat16
HEAD = 128
ROW = 4
DOCS = 8
FACTOR = 1.0 / math.sqrt(HEAD)
FACTOR2 = FACTOR * math.log2(math.e)
BIG = -1e30
PAD = 16


def dot_nt(a, b):
    return lax.dot_general(a, b, (((1,), (1,)), ((), ())), preferred_element_type=F32)


def dot_nn(a, b):
    return lax.dot_general(a, b, (((1,), (0,)), ((), ())), preferred_element_type=F32)


def pick(index, values):
    out = values[-1]
    for i in range(len(values) - 2, -1, -1):
        out = jnp.where(index == i, values[i], out)
    return out


def kernel(
    n_seq, n_tp,
    q_in, k_in, v_in, do_in, doc,
    dq_out, dk_out, dv_out,
    q, do, dog, kbuf, vbuf, qs, gs, keysT,
    e_ref, p_ref, ds_ref, bias, qt, gt, peak_blk, w_blk, f_ref, peak, total, row_dot,
    pk, pv, rel, msg_a, msg_b, down, dk_v, dv_v, dq_v, dkv,
    in_sem, out_sem, do_send, do_recv, kv_send, kv_recv, rs_send, rs_recv,
):
    s = lax.axis_index("seq")
    t = lax.axis_index("tp")
    z = s // ROW
    y = lax.rem(s, ROW)
    rows = n_seq // ROW
    tokens, cols = q.shape
    heads = cols // HEAD
    rows_do = do.shape[0]
    right = {"seq": z * ROW + lax.rem(y + 1, ROW)}
    left = {"seq": z * ROW + lax.rem(y + ROW - 1, ROW)}
    opposite = {"seq": z * ROW + lax.rem(y + 2, ROW)}

    barrier = pltpu.get_barrier_semaphore()
    for d in range(1, n_tp):
        pl.semaphore_signal(barrier, inc=1, device_id={"tp": lax.rem(t + d, n_tp)}, device_id_type=MESH)
    near = [z * ROW + lax.rem(y + d, ROW) for d in (1, 2, 3)]
    near += [lax.rem(z + d, rows) * ROW + y for d in (1, 2, 3)]
    near += [lax.rem(z + 2, rows) * ROW + lax.rem(y + 2, ROW)]
    for n in near:
        pl.semaphore_signal(barrier, inc=1, device_id={"seq": n}, device_id_type=MESH)

    own = 8 + y
    loads = [
        pltpu.make_async_copy(k_in, kbuf.at[own, 0:tokens], in_sem.at[0]),
        pltpu.make_async_copy(v_in, vbuf.at[own], in_sem.at[1]),
        pltpu.make_async_copy(q_in, q, in_sem.at[2]),
        pltpu.make_async_copy(do_in, do, in_sem.at[3]),
    ]
    for c in loads:
        c.start()
    docf = doc[...].astype(F32)
    kbuf[own, tokens : tokens + PAD, :] = jnp.concatenate(
        [docf[:, 0:HEAD], docf[:, HEAD:], jnp.zeros((PAD - 2, HEAD), F32)], axis=0
    ).astype(BF16)
    for r in range(2):

        @pl.when(z + r < 2)
        def _():
            for i in range(ROW):
                kbuf[r * ROW + i, 0:tokens, :] = jnp.zeros((tokens, HEAD), BF16)
                kbuf[r * ROW + i, tokens : tokens + PAD, :] = jnp.full((PAD, HEAD), -1.0, BF16)
                vbuf[r * ROW + i, :, :] = jnp.zeros((tokens, HEAD), BF16)

    for c in loads:
        c.wait()
    pl.semaphore_wait(barrier, n_tp - 1 + len(near))

    started = []

    def send(when, src, dst, ssem, rsem, to):
        def make():
            return pltpu.make_async_remote_copy(src(), dst(), ssem(), rsem(), device_id=to, device_id_type=MESH)

        @pl.when(when())
        def _():
            make().start()

        started.append((when, make))

    def send_block(when, slot, dst_slot, half, index, to):
        buf = (kbuf, vbuf)[half]
        send(
            when, lambda: buf.at[slot], lambda: buf.at[dst_slot],
            lambda: kv_send.at[index], lambda: kv_recv.at[2 * dst_slot + half], to,
        )

    def wait_block(when, slot, halves=(0, 1)):
        for half in halves:
            buf = (kbuf, vbuf)[half]

            @pl.when(when)
            def _():
                pltpu.make_async_remote_copy(
                    buf.at[slot], buf.at[slot], kv_send.at[0], kv_recv.at[2 * slot + half],
                    device_id=right, device_id_type=MESH,
                ).wait_recv()

    has1, has2 = z >= 1, z >= 2
    for half in range(2):
        send_block(lambda: z + 1 < rows, own, 4 + y, half, half, {"seq": lax.rem(s + ROW, n_seq)})
    below2 = lax.rem(z + 2, rows) * ROW
    for half in range(2):
        send_block(lambda: y <= 2, own, own, half, 2 + half, right)
        send_block(lambda: y == 0, own, own, half, 4 + half, left)
        send_block(lambda: y <= 1, own, own, half, 6 + half, opposite)
    for half in range(2):
        send_block(lambda: z + 2 < rows, own, y, half, 8 + half, {"seq": below2 + y})
    for half in range(2):
        send_block(
            lambda: (z + 2 < rows) & (y >= 2), own, y, half, 10 + half,
            {"seq": below2 + lax.rem(y + 2, ROW)},
        )
    do_copies = []
    for d in (2, 6, 4, 3, 5, 7, 1):
        p = lax.rem(t + d, n_tp)
        c = pltpu.make_async_remote_copy(
            do.at[:, pl.ds(pl.multiple_of(p * cols, cols), cols)],
            dog.at[pl.ds(pl.multiple_of(t * rows_do, rows_do), rows_do), :],
            do_send.at[d - 1],
            do_recv.at[d - 1],
            device_id={"tp": p},
            device_id_type=MESH,
        )
        c.start()
        do_copies.append(c)
    dog[pl.ds(pl.multiple_of(t * rows_do, rows_do), rows_do), :] = do[
        :, pl.ds(pl.multiple_of(t * cols, cols), cols)
    ]

    col1, own_left, y1, y2 = 4 + y, own - 1, y + 1, y + 2
    slots_a = [jnp.where(y + e < ROW, y + e, y + e + 4) for e in range(4)]
    slots_b = [4 + lax.rem(y + e, ROW) for e in range(4)]
    to1 = {"seq": lax.rem(s + n_seq - ROW, n_seq)}
    to2 = {"seq": lax.rem(s + n_seq - 2 * ROW, n_seq)}

    def slot_a(e):
        return slots_a[e]

    def slot_b(e):
        return slots_b[e]

    key_at = lax.broadcasted_iota(jnp.int32, (tokens, tokens), 0)
    query_at = lax.broadcasted_iota(jnp.int32, (tokens, tokens), 1)

    def head_rows(h):
        return pl.ds(pl.multiple_of(h * tokens, tokens), tokens)

    for h in range(heads):
        qs[h * tokens : (h + 1) * tokens, :] = q[:, h * HEAD : (h + 1) * HEAD]

    def scores(slot, diagonal):
        w = slot - y
        kb = kbuf[slot, 0:tokens, :]
        docs = kbuf[slot, tokens : tokens + PAD, :].astype(F32)[0:2, :]
        low = jnp.zeros((1, tokens), F32)
        for d in range(DOCS):
            count = jnp.sum(jnp.where(docs < d, 1.0, 0.0), axis=(0, 1), keepdims=True)
            low = low + jnp.where(docf == d, count, 0.0)
        seen = key_at >= low.astype(jnp.int32)
        if diagonal:
            seen = seen & (key_at <= query_at)
        bias[...] = jnp.where(seen, 0.0, BIG)

        def one(h, c):
            sc = dot_nt(kb, qs[head_rows(h), :]) + bias[...]
            top = jnp.max(sc, axis=0, keepdims=True)
            if not diagonal:
                old = peak[h]
                top = jnp.maximum(old, top)
            e = jnp.exp2((sc - top) * FACTOR2)
            part = jnp.sum(e, axis=0, keepdims=True)
            if not diagonal:
                part = part + total[h] * jnp.exp2((old - top) * FACTOR2)
            total[h] = part
            peak[h] = top
            peak_blk[w, h] = top
            e_ref[w, h] = e
            return c

        lax.fori_loop(0, heads, one, 0, unroll=heads)

    def here(slot):
        return jnp.where(slot >= 8, True, jnp.where(slot >= 4, has1, has2))

    def weight_grads(slot):
        w = slot - y
        known = (slot == own) | (slot == 4 + y) | (slot == y) | (slot == slot_b(1))
        wait_block(here(slot) & jnp.logical_not(known), slot, (1,))
        vb = vbuf[slot]

        def one(h, c):
            dp = dot_nt(vb, gs[head_rows(h), :])
            p_ref[w, h] = dp
            w_blk[w, h] = jnp.sum(e_ref[w, h] * dp, axis=0, keepdims=True)
            return c

        lax.fori_loop(0, heads, one, 0, unroll=heads)

    scores(own, True)
    for h in range(heads):
        qt[:, h * tokens : (h + 1) * tokens] = q[:, h * HEAD : (h + 1) * HEAD].T

    def first_stage():
        for half in range(2):
            wait_block(has1, 4 + y, (half,))
            send_block(lambda: has1, col1, col1, half, 12 + half, right)
            send_block(lambda: has1, col1, col1, half, 14 + half, left)

    def step_slot(k):
        late = k - 6 - y
        return pick(
            k,
            [
                own,
                4 + y,
                *[
                    jnp.where(
                        k < 2 + y,
                        pick(y, [8, 8, jnp.where(k == 2, 9, 8), jnp.where(k == 2, 10, jnp.where(k == 3, 8, 9))]),
                        jnp.where(
                            k < 6 + y,
                            pick(k - 2 - y, [y, slot_b(3), slot_b(1), slot_b(2)]),
                            pick(y, [pick(late, [1, 3, 2]), pick(late, [2, 3]), 3, 3]),
                        ),
                    )
                ]
                * 7,
            ],
        )

    first_stage()

    def gather_do():
        for c in do_copies:
            c.wait_recv()
        for h in range(heads):
            gs[h * tokens : (h + 1) * tokens, :] = dog[:, h * HEAD : (h + 1) * HEAD]
            gt[:, h * tokens : (h + 1) * tokens] = dog[:, h * HEAD : (h + 1) * HEAD].T

    def loop(k, c):
        @pl.when(k == jnp.minimum(2 + y, 3))
        def _():
            for half in range(2):
                wait_block(has2, y, (half,))
                send_block(lambda: has2 & (y == 3), y, y, half, 16 + half, right)
                send_block(lambda: has2 & (y >= 1), y, y, half, 18 + half, left)

        @pl.when(k == jnp.minimum(3 + y, 4))
        def _():
            wait_block(has1, slot_b(3), (0,))
            send_block(lambda: has1, slot_b(3), slot_b(3), 0, 20, right)
            wait_block(has1, slot_b(1), (1,))
            send_block(lambda: has1, slot_b(1), slot_b(1), 1, 21, left)

        @pl.when(k == 6)
        def _():
            gather_do()

            def early(j, c):
                weight_grads(step_slot(j))
                return c

            lax.fori_loop(0, 6, early, 0)

        slot = step_slot(k)
        known = (slot == own) | (slot == 4 + y) | (slot == y) | (slot == slot_b(3))
        wait_block(here(slot) & jnp.logical_not(known), slot, (0,))
        scores(slot, False)
        return c

    lax.fori_loop(1, 9, loop, 0)

    def rest(j, c):
        weight_grads(step_slot(j))
        return c

    lax.fori_loop(6, 9, rest, 0)

    def stats(h, c):
        inv = 1.0 / total[h]
        acc = jnp.zeros((1, tokens), F32)
        for w in range(9):
            f = jnp.exp2((peak_blk[w, h] - peak[h]) * FACTOR2) * inv
            f_ref[w, h] = f
            acc = acc + f * w_blk[w, h]
        row_dot[h] = acc
        return c

    lax.fori_loop(0, heads, stats, 0)

    order = [slot_b(2), slot_a(2), slot_b(1), slot_b(3), slot_a(1), slot_a(3), y, 4 + y, own]
    halves = (pk, pv)

    def rs(when, src, dst, index, to):
        send(when, src, dst, lambda: rs_send.at[index], lambda: rs_recv.at[index], to)

    def rs_wait(when, dst, index):
        @pl.when(when)
        def _():
            pltpu.make_async_remote_copy(
                dst, dst, rs_send.at[index], rs_recv.at[index], device_id=right, device_id_type=MESH
            ).wait_recv()

    def add(when, half, slot, other):
        @pl.when(when)
        def _():
            halves[half][slot] = (halves[half][slot].astype(F32) + other[...].astype(F32)).astype(BF16)

    a2_any = has2 | (y >= 2)
    a1_any = has2 | (y == 3)
    a3_any = has2 | (y >= 1)

    def after(j):
        if j == 0:
            rs(lambda: has1, lambda: pk.at[slot_b(2)], lambda: rel.at[0], 0, right)
            rs(lambda: has1, lambda: pv.at[slot_b(2)], lambda: rel.at[1], 1, left)
        if j == 1:
            sl = slot_a(2)
            rs(lambda: has2 & (y == 0), lambda: pk.at[sl], lambda: rel.at[2], 2, right)
            rs(lambda: a2_any & (y >= 1), lambda: pk.at[sl], lambda: rel.at[3], 3, left)
            rs(lambda: a2_any & (y <= 2), lambda: pv.at[sl], lambda: rel.at[4], 4, right)
            rs(lambda: y == 3, lambda: pv.at[sl], lambda: rel.at[5], 5, left)
        if j == 2:
            rs(lambda: has1, lambda: pv.at[slot_b(1)], lambda: msg_b.at[1], 7, right)
        if j == 3:
            rs(lambda: has1, lambda: pk.at[slot_b(3)], lambda: msg_b.at[2], 8, left)
            rs_wait(has1, rel.at[0], 0)
            add(has1, 0, slot_b(1), rel.at[0])
            rs(lambda: has1, lambda: pk.at[slot_b(1)], lambda: msg_b.at[0], 6, right)
            rs_wait(has1, rel.at[1], 1)
            add(has1, 1, slot_b(3), rel.at[1])
            rs(lambda: has1, lambda: pv.at[slot_b(3)], lambda: msg_b.at[3], 9, left)
        if j == 4:
            sl = slot_a(1)
            rs_wait(has2 & (y == 1), rel.at[2], 2)
            add(has2 & (y == 1), 0, sl, rel.at[2])
            rs(lambda: a1_any, lambda: pk.at[sl], lambda: msg_a.at[0], 10, right)
            got_v = (has2 & (y >= 1)) | (y == 3)
            rs_wait(got_v, rel.at[4], 4)
            add(got_v, 1, sl, rel.at[4])
            rs(lambda: a1_any, lambda: pv.at[sl], lambda: msg_a.at[1], 11, right)
        if j == 5:
            sl = slot_a(3)
            got_k = (has2 & (y == 0)) | (y == 1) | (y == 2)
            rs_wait(got_k, rel.at[3], 3)
            add(got_k, 0, sl, rel.at[3])
            rs(lambda: a3_any, lambda: pk.at[sl], lambda: msg_a.at[2], 12, left)
            rs_wait(y == 2, rel.at[5], 5)
            add(y == 2, 1, sl, rel.at[5])
            rs(lambda: a3_any, lambda: pv.at[sl], lambda: msg_a.at[3], 13, left)
        if j == 7:
            for half in range(2):
                rs_wait(has1, msg_b.at[half], 6 + half)
                add(has1, half, 4 + y, msg_b.at[half])
                rs_wait(has1, msg_b.at[2 + half], 8 + half)
                add(has1, half, 4 + y, msg_b.at[2 + half])
                rs(lambda: has1, lambda half=half: halves[half].at[col1], lambda half=half: down.at[half], 14 + half, to1)
            from_left = (has2 & (y >= 1)) | (y == 0)
            from_right = (has2 & (y == 3)) | (y <= 2)
            for half in range(2):
                rs_wait(from_left, msg_a.at[half], 10 + half)
                rs_wait(from_right, msg_a.at[2 + half], 12 + half)
                add(has2 & (y >= 1), half, y, msg_a.at[half])
                add(has2 & (y == 3), half, y, msg_a.at[2 + half])
                rs(lambda: has2, lambda half=half: halves[half].at[y], lambda half=half: down.at[2 + half], 16 + half, to2)

    def block_grads(j):
        slot = pick(j, order)
        w = slot - y
        dvt = jnp.zeros((HEAD, tokens), F32)
        dkt = jnp.zeros((HEAD, tokens), F32)
        for h in range(heads):
            hs = slice(h * tokens, (h + 1) * tokens)
            p = e_ref[w, h] * f_ref[w, h]
            ds = (p * (p_ref[w, h] - row_dot[h])).astype(BF16)
            ds_ref[w, h] = ds
            dvt = dvt + dot_nt(gt[:, hs], p.astype(BF16))
            dkt = dkt + dot_nt(qt[:, hs], ds)
        dkt = dkt * FACTOR
        pk[slot] = dkt.astype(BF16)
        pv[slot] = dvt.astype(BF16)

        @pl.when(j == 8)
        def _():
            dkv[0] = dkt
            dkv[1] = dvt

    def grads(j, c):
        block_grads(j)
        for i in range(8):

            @pl.when(j == i)
            def _():
                after(i)

        return c

    lax.fori_loop(0, 9, grads, 0)

    for w in range(9):
        keysT[:, w * tokens : (w + 1) * tokens] = kbuf[y + w, 0:tokens, :].astype(F32).T.astype(BF16)

    def query(h, c):
        acc = jnp.zeros((HEAD, tokens), F32)
        for w in range(9):
            acc = acc + dot_nn(keysT[:, w * tokens : (w + 1) * tokens], ds_ref[w, h])
        dq_v[:, pl.ds(pl.multiple_of(h * HEAD, HEAD), HEAD)] = (acc.T * FACTOR).astype(BF16)
        return c

    lax.fori_loop(0, heads, query, 0)
    dq_copy = pltpu.make_async_copy(dq_v, dq_out, out_sem.at[0])
    dq_copy.start()

    for half in range(2):

        @pl.when(y == 0)
        def _():
            dkv[half] += msg_a[half].astype(F32)

        @pl.when(y <= 2)
        def _():
            dkv[half] += msg_a[2 + half].astype(F32)

    for i, when in ((0, z + 1 < rows), (2, z + 2 < rows)):
        for half in range(2):
            rs_wait(when, down.at[i + half], 14 + i + half)

            @pl.when(when)
            def _():
                dkv[half] += down[i + half].astype(F32)

    dk_v[...] = dkv[0].T.astype(BF16)
    dv_v[...] = dkv[1].T.astype(BF16)
    outs = [
        pltpu.make_async_copy(dk_v, dk_out, out_sem.at[1]),
        pltpu.make_async_copy(dv_v, dv_out, out_sem.at[2]),
    ]
    for c in outs:
        c.start()
    for c in do_copies:
        c.wait_send()
    for when, make in started:

        @pl.when(when())
        def _():
            make().wait_send()

    for c in outs:
        c.wait()
    dq_copy.wait()


def solution(mesh):
    n_seq, n_tp = mesh.shape["seq"], mesh.shape["tp"]

    def local(queries, key_matrix, value_matrix, output_gradient, document):
        tokens, cols = queries.shape
        heads = cols // HEAD
        hbm = pl.BlockSpec(memory_space=pltpu.HBM)
        vm = pl.BlockSpec(memory_space=pltpu.VMEM)
        dma = pltpu.SemaphoreType.DMA
        v = pltpu.VMEM
        return pl.pallas_call(
            functools.partial(kernel, n_seq, n_tp),
            out_shape=[
                jax.ShapeDtypeStruct((tokens, cols), BF16),
                jax.ShapeDtypeStruct((tokens, HEAD), BF16),
                jax.ShapeDtypeStruct((tokens, HEAD), BF16),
            ],
            in_specs=[hbm] * 4 + [vm],
            out_specs=[hbm] * 3,
            scratch_shapes=[
                v((tokens, cols), BF16),
                v(output_gradient.shape, BF16),
                v((tokens, cols), BF16),
                v((12, tokens + PAD, HEAD), BF16),
                v((12, tokens, HEAD), BF16),
                v((heads * tokens, HEAD), BF16),
                v((heads * tokens, HEAD), BF16),
                v((HEAD, 9 * tokens), BF16),
                v((9, heads, tokens, tokens), F32),
                v((9, heads, tokens, tokens), F32),
                v((9, heads, tokens, tokens), BF16),
                v((tokens, tokens), F32),
                v((HEAD, heads * tokens), BF16),
                v((HEAD, heads * tokens), BF16),
                v((9, heads, 1, tokens), F32),
                v((9, heads, 1, tokens), F32),
                v((9, heads, 1, tokens), F32),
                v((heads, 1, tokens), F32),
                v((heads, 1, tokens), F32),
                v((heads, 1, tokens), F32),
                v((12, HEAD, tokens), BF16),
                v((12, HEAD, tokens), BF16),
                v((6, HEAD, tokens), BF16),
                v((4, HEAD, tokens), BF16),
                v((4, HEAD, tokens), BF16),
                v((4, HEAD, tokens), BF16),
                v((tokens, HEAD), BF16),
                v((tokens, HEAD), BF16),
                v((tokens, cols), BF16),
                v((2, HEAD, tokens), F32),
                dma((4,)), dma((3,)), dma((n_tp - 1,)), dma((n_tp - 1,)),
                dma((24,)), dma((24,)), dma((18,)), dma((18,)),
            ],
            compiler_params=pltpu.CompilerParams(
                collective_id=0, has_side_effects=True, vmem_limit_bytes=63 * 1024 * 1024
            ),
        )(queries, key_matrix, value_matrix, output_gradient, document.reshape(1, tokens))

    return jax.shard_map(
        local,
        mesh=mesh,
        in_specs=(P("seq", "tp"), P("seq", "tp"), P("seq", "tp"), P(("seq", "tp"), None), P("seq")),
        out_specs=(P("seq", "tp"),) * 3,
        check_vma=False,
    )
```

```python
import functools
import math

import jax
import jax.numpy as jnp
from jax import lax
from jax.experimental import pallas as pl
from jax.experimental.pallas import tpu as pltpu
from jax.sharding import PartitionSpec as P

MESH = pl.DeviceIdType.MESH
F32 = jnp.float32
BF16 = jnp.bfloat16
HEAD = 128
ROW = 4
DOCS = 8
FACTOR = 1.0 / math.sqrt(HEAD)
FACTOR2 = FACTOR * math.log2(math.e)
BIG = -1e30
PAD = 16


def dot_nt(a, b):
    return lax.dot_general(a, b, (((1,), (1,)), ((), ())), preferred_element_type=F32)


def dot_nn(a, b):
    return lax.dot_general(a, b, (((1,), (0,)), ((), ())), preferred_element_type=F32)


def pick(index, values):
    out = values[-1]
    for i in range(len(values) - 2, -1, -1):
        out = jnp.where(index == i, values[i], out)
    return out


def kernel(
    n_seq, n_tp,
    q_in, k_in, v_in, do_in, doc,
    dq_out, dk_out, dv_out,
    q, do, dog, kbuf, vbuf, qs, gs, keysT,
    e_ref, p_ref, ds_ref, bias, qt, gt, peak_blk, w_blk, f_ref, peak, total, row_dot,
    pk, pv, rel, msg_a, msg_b, down, dkv,
    kvia, vvia, via_send, via_recv, in_sem, do_send, do_recv, kv_send, kv_recv, rs_send, rs_recv,
):
    s = lax.axis_index("seq")
    t = lax.axis_index("tp")
    z = s // ROW
    y = lax.rem(s, ROW)
    rows = n_seq // ROW
    tokens, cols = q.shape
    heads = cols // HEAD
    rows_do = do.shape[0]
    right = {"seq": z * ROW + lax.rem(y + 1, ROW)}
    left = {"seq": z * ROW + lax.rem(y + ROW - 1, ROW)}
    below = {"seq": lax.rem(z + 2, rows) * ROW + y}
    opposite = {"seq": z * ROW + lax.rem(y + 2, ROW)}

    barrier = pltpu.get_barrier_semaphore()
    for d in range(1, n_tp):
        pl.semaphore_signal(barrier, inc=1, device_id={"tp": lax.rem(t + d, n_tp)}, device_id_type=MESH)
    near = [z * ROW + lax.rem(y + d, ROW) for d in (1, 2, 3)]
    near += [lax.rem(z + d, rows) * ROW + y for d in (1, 2, 3)]
    for n in near:
        pl.semaphore_signal(barrier, inc=1, device_id={"seq": n}, device_id_type=MESH)

    own = 8 + y
    loads = [
        pltpu.make_async_copy(k_in, kbuf.at[own, 0:tokens], in_sem.at[0]),
        pltpu.make_async_copy(v_in, vbuf.at[own], in_sem.at[1]),
        pltpu.make_async_copy(q_in, q, in_sem.at[2]),
        pltpu.make_async_copy(do_in, do, in_sem.at[3]),
    ]
    for c in loads:
        c.start()
    docf = doc[...].astype(F32)
    kbuf[own, tokens : tokens + PAD, :] = jnp.concatenate(
        [docf[:, 0:HEAD], docf[:, HEAD:], jnp.zeros((PAD - 2, HEAD), F32)], axis=0
    ).astype(BF16)
    for r in range(2):

        @pl.when(z + r < 2)
        def _():
            for i in range(ROW):
                kbuf[r * ROW + i, 0:tokens, :] = jnp.zeros((tokens, HEAD), BF16)
                kbuf[r * ROW + i, tokens : tokens + PAD, :] = jnp.full((PAD, HEAD), -1.0, BF16)
                vbuf[r * ROW + i, :, :] = jnp.zeros((tokens, HEAD), BF16)

    for c in loads:
        c.wait()
    pl.semaphore_wait(barrier, n_tp - 1 + len(near))

    started = []

    def send(when, src, dst, ssem, rsem, to):
        def make():
            return pltpu.make_async_remote_copy(src(), dst(), ssem(), rsem(), device_id=to, device_id_type=MESH)

        @pl.when(when())
        def _():
            make().start()

        started.append((when, make))

    def send_block(when, slot, dst_slot, half, index, to):
        buf = (kbuf, vbuf)[half]
        send(
            when, lambda: buf.at[slot], lambda: buf.at[dst_slot],
            lambda: kv_send.at[index], lambda: kv_recv.at[2 * dst_slot + half], to,
        )

    def wait_block(when, slot, halves=(0, 1)):
        for half in halves:
            buf = (kbuf, vbuf)[half]

            @pl.when(when)
            def _():
                pltpu.make_async_remote_copy(
                    buf.at[slot], buf.at[slot], kv_send.at[0], kv_recv.at[2 * slot + half],
                    device_id=right, device_id_type=MESH,
                ).wait_recv()

    has1, has2 = z >= 1, z >= 2
    for half in range(2):
        send_block(lambda: z + 1 < rows, own, 4 + y, half, half, {"seq": lax.rem(s + ROW, n_seq)})
    for half in range(2):
        send_block(lambda: y <= 2, own, own, half, 2 + half, right)
        send_block(lambda: y == 0, own, own, half, 4 + half, left)
        send_block(lambda: y <= 1, own, own, half, 6 + half, opposite)
    for half in range(2):
        send_block(lambda: z + 2 < rows, own, y, half, 8 + half, below)
    for half in range(2):
        send(
            lambda: (z + 2 < rows) & (y >= 2),
            lambda half=half: (kbuf, vbuf)[half].at[own],
            lambda half=half: (kvia, vvia)[half],
            lambda half=half: via_send.at[half],
            lambda half=half: via_recv.at[half],
            opposite,
        )
    do_copies = []
    for d in (2, 6, 4, 3, 5, 7, 1):
        p = lax.rem(t + d, n_tp)
        c = pltpu.make_async_remote_copy(
            do.at[:, pl.ds(pl.multiple_of(p * cols, cols), cols)],
            dog.at[pl.ds(pl.multiple_of(t * rows_do, rows_do), rows_do), :],
            do_send.at[d - 1],
            do_recv.at[d - 1],
            device_id={"tp": p},
            device_id_type=MESH,
        )
        c.start()
        do_copies.append(c)
    dog[pl.ds(pl.multiple_of(t * rows_do, rows_do), rows_do), :] = do[
        :, pl.ds(pl.multiple_of(t * cols, cols), cols)
    ]

    col1, own_left, y1, y2 = 4 + y, own - 1, y + 1, y + 2
    slots_a = [jnp.where(y + e < ROW, y + e, y + e + 4) for e in range(4)]
    slots_b = [4 + lax.rem(y + e, ROW) for e in range(4)]
    to1 = {"seq": lax.rem(s + n_seq - ROW, n_seq)}
    to2 = {"seq": lax.rem(s + n_seq - 2 * ROW, n_seq)}

    def slot_a(e):
        return slots_a[e]

    def slot_b(e):
        return slots_b[e]

    key_at = lax.broadcasted_iota(jnp.int32, (tokens, tokens), 0)
    query_at = lax.broadcasted_iota(jnp.int32, (tokens, tokens), 1)

    def head_rows(h):
        return pl.ds(pl.multiple_of(h * tokens, tokens), tokens)

    for h in range(heads):
        qs[h * tokens : (h + 1) * tokens, :] = q[:, h * HEAD : (h + 1) * HEAD]

    def scores(slot, diagonal):
        w = slot - y
        kb = kbuf[slot, 0:tokens, :]
        docs = kbuf[slot, tokens : tokens + PAD, :].astype(F32)[0:2, :]
        low = jnp.zeros((1, tokens), F32)
        for d in range(DOCS):
            count = jnp.sum(jnp.where(docs < d, 1.0, 0.0), axis=(0, 1), keepdims=True)
            low = low + jnp.where(docf == d, count, 0.0)
        seen = key_at >= low.astype(jnp.int32)
        if diagonal:
            seen = seen & (key_at <= query_at)
        bias[...] = jnp.where(seen, 0.0, BIG)

        def one(h, c):
            sc = dot_nt(kb, qs[head_rows(h), :]) + bias[...]
            top = jnp.max(sc, axis=0, keepdims=True)
            if not diagonal:
                old = peak[h]
                top = jnp.maximum(old, top)
            e = jnp.exp2((sc - top) * FACTOR2)
            part = jnp.sum(e, axis=0, keepdims=True)
            if not diagonal:
                part = part + total[h] * jnp.exp2((old - top) * FACTOR2)
            total[h] = part
            peak[h] = top
            peak_blk[w, h] = top
            e_ref[w, h] = e
            return c

        lax.fori_loop(0, heads, one, 0, unroll=heads)

    def here(slot):
        return jnp.where(slot >= 8, True, jnp.where(slot >= 4, has1, has2))

    def weight_grads(slot):
        w = slot - y
        known = (slot == own) | (slot == 4 + y) | (slot == y) | (slot == slot_b(1))
        wait_block(here(slot) & jnp.logical_not(known), slot, (1,))
        vb = vbuf[slot]

        def one(h, c):
            dp = dot_nt(vb, gs[head_rows(h), :])
            p_ref[w, h] = dp
            w_blk[w, h] = jnp.sum(e_ref[w, h] * dp, axis=0, keepdims=True)
            return c

        lax.fori_loop(0, heads, one, 0, unroll=heads)

    scores(own, True)
    for h in range(heads):
        qt[:, h * tokens : (h + 1) * tokens] = q[:, h * HEAD : (h + 1) * HEAD].T

    def first_stage():
        for half in range(2):
            wait_block(has1, 4 + y, (half,))
            send_block(lambda: has1, col1, col1, half, 12 + half, right)
            send_block(lambda: has1, col1, col1, half, 14 + half, left)

    def step_slot(k):
        late = k - 6 - y
        return pick(
            k,
            [
                own,
                4 + y,
                *[
                    jnp.where(
                        k < 2 + y,
                        pick(y, [8, 8, jnp.where(k == 2, 9, 8), jnp.where(k == 2, 10, jnp.where(k == 3, 8, 9))]),
                        jnp.where(
                            k < 6 + y,
                            pick(k - 2 - y, [y, slot_b(3), slot_b(1), slot_b(2)]),
                            pick(y, [pick(late, [1, 3, 2]), pick(late, [2, 3]), 3, 3]),
                        ),
                    )
                ]
                * 7,
            ],
        )

    first_stage()

    def gather_do():
        for c in do_copies:
            c.wait_recv()
        for h in range(heads):
            gs[h * tokens : (h + 1) * tokens, :] = dog[:, h * HEAD : (h + 1) * HEAD]
            gt[:, h * tokens : (h + 1) * tokens] = dog[:, h * HEAD : (h + 1) * HEAD].T

    def loop(k, c):
        @pl.when(k == jnp.minimum(2 + y, 3))
        def _():
            for half in range(2):
                via = (kvia, vvia)[half]

                @pl.when((z + 2 < rows) & (y <= 1))
                def _():
                    pltpu.make_async_remote_copy(
                        via, via, via_send.at[half], via_recv.at[half], device_id=right, device_id_type=MESH
                    ).wait_recv()

                send(
                    lambda: (z + 2 < rows) & (y <= 1),
                    lambda half=half: (kvia, vvia)[half],
                    lambda half=half: (kbuf, vbuf)[half].at[y2],
                    lambda half=half: kv_send.at[10 + half],
                    lambda half=half: kv_recv.at[2 * y2 + half],
                    below,
                )

            for half in range(2):
                wait_block(has2, y, (half,))
                send_block(lambda: has2 & (y == 3), y, y, half, 16 + half, right)
                send_block(lambda: has2 & (y >= 1), y, y, half, 18 + half, left)

        @pl.when(k == jnp.minimum(3 + y, 4))
        def _():
            wait_block(has1, slot_b(3), (0,))
            send_block(lambda: has1, slot_b(3), slot_b(3), 0, 20, right)
            wait_block(has1, slot_b(1), (1,))
            send_block(lambda: has1, slot_b(1), slot_b(1), 1, 21, left)

        @pl.when(k == 5 + y)
        def _():
            gather_do()

            def early(j, c):
                weight_grads(step_slot(j))
                return c

            lax.fori_loop(0, 5 + y, early, 0)

        slot = step_slot(k)
        known = (slot == own) | (slot == 4 + y) | (slot == y) | (slot == slot_b(3))
        wait_block(here(slot) & jnp.logical_not(known), slot, (0,))
        scores(slot, False)
        return c

    lax.fori_loop(1, 9, loop, 0)

    def rest(j, c):
        weight_grads(step_slot(j))
        return c

    lax.fori_loop(5 + y, 9, rest, 0)

    def stats(h, c):
        inv = 1.0 / total[h]
        acc = jnp.zeros((1, tokens), F32)
        for w in range(9):
            f = jnp.exp2((peak_blk[w, h] - peak[h]) * FACTOR2) * inv
            f_ref[w, h] = f
            acc = acc + f * w_blk[w, h]
        row_dot[h] = acc
        return c

    lax.fori_loop(0, heads, stats, 0)

    order = [slot_b(2), slot_a(2), slot_b(1), slot_b(3), slot_a(1), slot_a(3), y, 4 + y, own]
    halves = (pk, pv)

    def rs(when, src, dst, index, to):
        send(when, src, dst, lambda: rs_send.at[index], lambda: rs_recv.at[index], to)

    def rs_wait(when, dst, index):
        @pl.when(when)
        def _():
            pltpu.make_async_remote_copy(
                dst, dst, rs_send.at[index], rs_recv.at[index], device_id=right, device_id_type=MESH
            ).wait_recv()

    def add(when, half, slot, other):
        @pl.when(when)
        def _():
            halves[half][slot] = (halves[half][slot].astype(F32) + other[...].astype(F32)).astype(BF16)

    a2_any = has2 | (y >= 2)
    a1_any = has2 | (y == 3)
    a3_any = has2 | (y >= 1)

    def after(j):
        if j == 0:
            rs(lambda: has1, lambda: pk.at[slot_b(2)], lambda: rel.at[0], 0, right)
            rs(lambda: has1, lambda: pv.at[slot_b(2)], lambda: rel.at[1], 1, left)
        if j == 1:
            sl = slot_a(2)
            rs(lambda: has2 & (y == 0), lambda: pk.at[sl], lambda: rel.at[2], 2, right)
            rs(lambda: a2_any & (y >= 1), lambda: pk.at[sl], lambda: rel.at[3], 3, left)
            rs(lambda: a2_any & (y <= 2), lambda: pv.at[sl], lambda: rel.at[4], 4, right)
            rs(lambda: y == 3, lambda: pv.at[sl], lambda: rel.at[5], 5, left)
        if j == 2:
            rs(lambda: has1, lambda: pv.at[slot_b(1)], lambda: msg_b.at[1], 7, right)
        if j == 3:
            rs(lambda: has1, lambda: pk.at[slot_b(3)], lambda: msg_b.at[2], 8, left)
            rs_wait(has1, rel.at[0], 0)
            add(has1, 0, slot_b(1), rel.at[0])
            rs(lambda: has1, lambda: pk.at[slot_b(1)], lambda: msg_b.at[0], 6, right)
            rs_wait(has1, rel.at[1], 1)
            add(has1, 1, slot_b(3), rel.at[1])
            rs(lambda: has1, lambda: pv.at[slot_b(3)], lambda: msg_b.at[3], 9, left)
        if j == 4:
            sl = slot_a(1)
            rs_wait(has2 & (y == 1), rel.at[2], 2)
            add(has2 & (y == 1), 0, sl, rel.at[2])
            rs(lambda: a1_any, lambda: pk.at[sl], lambda: msg_a.at[0], 10, right)
            got_v = (has2 & (y >= 1)) | (y == 3)
            rs_wait(got_v, rel.at[4], 4)
            add(got_v, 1, sl, rel.at[4])
            rs(lambda: a1_any, lambda: pv.at[sl], lambda: msg_a.at[1], 11, right)
        if j == 5:
            sl = slot_a(3)
            got_k = (has2 & (y == 0)) | (y == 1) | (y == 2)
            rs_wait(got_k, rel.at[3], 3)
            add(got_k, 0, sl, rel.at[3])
            rs(lambda: a3_any, lambda: pk.at[sl], lambda: msg_a.at[2], 12, left)
            rs_wait(y == 2, rel.at[5], 5)
            add(y == 2, 1, sl, rel.at[5])
            rs(lambda: a3_any, lambda: pv.at[sl], lambda: msg_a.at[3], 13, left)
        if j == 7:
            for half in range(2):
                rs_wait(has1, msg_b.at[half], 6 + half)
                add(has1, half, 4 + y, msg_b.at[half])
                rs_wait(has1, msg_b.at[2 + half], 8 + half)
                add(has1, half, 4 + y, msg_b.at[2 + half])
                rs(lambda: has1, lambda half=half: halves[half].at[col1], lambda half=half: down.at[half], 14 + half, to1)
            from_left = (has2 & (y >= 1)) | (y == 0)
            from_right = (has2 & (y == 3)) | (y <= 2)
            for half in range(2):
                rs_wait(from_left, msg_a.at[half], 10 + half)
                rs_wait(from_right, msg_a.at[2 + half], 12 + half)
                add(has2 & (y >= 1), half, y, msg_a.at[half])
                add(has2 & (y == 3), half, y, msg_a.at[2 + half])
                rs(lambda: has2, lambda half=half: halves[half].at[y], lambda half=half: down.at[2 + half], 16 + half, to2)

    def block_grads(j):
        slot = pick(j, order)
        w = slot - y
        dvt = jnp.zeros((HEAD, tokens), F32)
        dkt = jnp.zeros((HEAD, tokens), F32)
        for h in range(heads):
            hs = slice(h * tokens, (h + 1) * tokens)
            p = e_ref[w, h] * f_ref[w, h]
            ds = (p * (p_ref[w, h] - row_dot[h])).astype(BF16)
            ds_ref[w, h] = ds
            dvt = dvt + dot_nt(gt[:, hs], p.astype(BF16))
            dkt = dkt + dot_nt(qt[:, hs], ds)
        dkt = dkt * FACTOR
        pk[slot] = dkt.astype(BF16)
        pv[slot] = dvt.astype(BF16)

        @pl.when(j == 8)
        def _():
            dkv[0] = dkt
            dkv[1] = dvt

    def grads(j, c):
        block_grads(j)
        for i in range(8):

            @pl.when(j == i)
            def _():
                after(i)

        return c

    lax.fori_loop(0, 9, grads, 0)

    for w in range(9):
        keysT[:, w * tokens : (w + 1) * tokens] = kbuf[y + w, 0:tokens, :].astype(F32).T.astype(BF16)

    def query(h, c):
        acc = jnp.zeros((HEAD, tokens), F32)
        for w in range(9):
            acc = acc + dot_nn(keysT[:, w * tokens : (w + 1) * tokens], ds_ref[w, h])
        dq_out[:, pl.ds(pl.multiple_of(h * HEAD, HEAD), HEAD)] = (acc.T * FACTOR).astype(BF16)
        return c

    lax.fori_loop(0, heads, query, 0)

    for half in range(2):

        @pl.when(y == 0)
        def _():
            dkv[half] += msg_a[half].astype(F32)

        @pl.when(y <= 2)
        def _():
            dkv[half] += msg_a[2 + half].astype(F32)

    for i, when in ((0, z + 1 < rows), (2, z + 2 < rows)):
        for half in range(2):
            rs_wait(when, down.at[i + half], 14 + i + half)

            @pl.when(when)
            def _():
                dkv[half] += down[i + half].astype(F32)

    dk_out[...] = dkv[0].T.astype(BF16)
    dv_out[...] = dkv[1].T.astype(BF16)
    for c in do_copies:
        c.wait_send()
    for when, make in started:

        @pl.when(when())
        def _():
            make().wait_send()


def write_out(a, b, c, a_out, b_out, c_out, sem):
    copies = [
        pltpu.make_async_copy(src, dst, sem.at[i])
        for i, (src, dst) in enumerate(((a, a_out), (b, b_out), (c, c_out)))
    ]
    for copy in copies:
        copy.start()
    for copy in copies:
        copy.wait()


def solution(mesh):
    n_seq, n_tp = mesh.shape["seq"], mesh.shape["tp"]

    def local(queries, key_matrix, value_matrix, output_gradient, document):
        tokens, cols = queries.shape
        heads = cols // HEAD
        hbm = pl.BlockSpec(memory_space=pltpu.HBM)
        vm = pl.BlockSpec(memory_space=pltpu.VMEM)
        dma = pltpu.SemaphoreType.DMA
        v = pltpu.VMEM
        grads = pl.pallas_call(
            functools.partial(kernel, n_seq, n_tp),
            out_shape=[
                jax.ShapeDtypeStruct((tokens, cols), BF16),
                jax.ShapeDtypeStruct((tokens, HEAD), BF16),
                jax.ShapeDtypeStruct((tokens, HEAD), BF16),
            ],
            in_specs=[hbm] * 4 + [vm],
            out_specs=[vm] * 3,
            scratch_shapes=[
                v((tokens, cols), BF16),
                v(output_gradient.shape, BF16),
                v((tokens, cols), BF16),
                v((12, tokens + PAD, HEAD), BF16),
                v((12, tokens, HEAD), BF16),
                v((heads * tokens, HEAD), BF16),
                v((heads * tokens, HEAD), BF16),
                v((HEAD, 9 * tokens), BF16),
                v((9, heads, tokens, tokens), F32),
                v((9, heads, tokens, tokens), F32),
                v((9, heads, tokens, tokens), BF16),
                v((tokens, tokens), F32),
                v((HEAD, heads * tokens), BF16),
                v((HEAD, heads * tokens), BF16),
                v((9, heads, 1, tokens), F32),
                v((9, heads, 1, tokens), F32),
                v((9, heads, 1, tokens), F32),
                v((heads, 1, tokens), F32),
                v((heads, 1, tokens), F32),
                v((heads, 1, tokens), F32),
                v((12, HEAD, tokens), BF16),
                v((12, HEAD, tokens), BF16),
                v((6, HEAD, tokens), BF16),
                v((4, HEAD, tokens), BF16),
                v((4, HEAD, tokens), BF16),
                v((4, HEAD, tokens), BF16),
                v((2, HEAD, tokens), F32),
                v((tokens + PAD, HEAD), BF16), v((tokens, HEAD), BF16), dma((2,)), dma((2,)),
                dma((4,)), dma((n_tp - 1,)), dma((n_tp - 1,)),
                dma((24,)), dma((24,)), dma((18,)), dma((18,)),
            ],
            compiler_params=pltpu.CompilerParams(
                collective_id=0, has_side_effects=True, vmem_limit_bytes=63 * 1024 * 1024
            ),
        )(queries, key_matrix, value_matrix, output_gradient, document.reshape(1, tokens))
        return pl.pallas_call(
            write_out,
            out_shape=[jax.ShapeDtypeStruct(g.shape, g.dtype) for g in grads],
            in_specs=[vm] * 3,
            out_specs=[hbm] * 3,
            scratch_shapes=[dma((3,))],
        )(*grads)

    return jax.shard_map(
        local,
        mesh=mesh,
        in_specs=(P("seq", "tp"), P("seq", "tp"), P("seq", "tp"), P(("seq", "tp"), None), P("seq")),
        out_specs=(P("seq", "tp"),) * 3,
        check_vma=False,
    )
```

```python
import functools
import math

import jax
import jax.numpy as jnp
from jax import lax
from jax.experimental import pallas as pl
from jax.experimental.pallas import tpu as pltpu
from jax.sharding import PartitionSpec as P

MESH = pl.DeviceIdType.MESH
F32 = jnp.float32
BF16 = jnp.bfloat16
HEAD = 128
ROW = 4
DOCS = 8
FACTOR = 1.0 / math.sqrt(HEAD)
FACTOR2 = FACTOR * math.log2(math.e)
BIG = -1e30
PAD = 16


def dot_nt(a, b):
    return lax.dot_general(a, b, (((1,), (1,)), ((), ())), preferred_element_type=F32)


def dot_nn(a, b):
    return lax.dot_general(a, b, (((1,), (0,)), ((), ())), preferred_element_type=F32)


def pick(index, values):
    out = values[-1]
    for i in range(len(values) - 2, -1, -1):
        out = jnp.where(index == i, values[i], out)
    return out


def kernel(
    n_seq, n_tp,
    q_in, k_in, v_in, do_in, doc,
    dq_out, dk_out, dv_out,
    q, do, dog, kbuf, vbuf, qs, gs, keysT,
    e_ref, p_ref, ds_ref, bias, qt, gt, peak_blk, w_blk, f_ref, peak, total, row_dot,
    pk, pv, rel, msg_a, msg_b, down, dkv,
    kvia, vvia, via_send, via_recv, in_sem, do_send, do_recv, kv_send, kv_recv, rs_send, rs_recv,
):
    s = lax.axis_index("seq")
    t = lax.axis_index("tp")
    z = s // ROW
    y = lax.rem(s, ROW)
    rows = n_seq // ROW
    tokens, cols = q.shape
    heads = cols // HEAD
    rows_do = do.shape[0]
    right = {"seq": z * ROW + lax.rem(y + 1, ROW)}
    left = {"seq": z * ROW + lax.rem(y + ROW - 1, ROW)}
    below = {"seq": lax.rem(z + 2, rows) * ROW + y}
    opposite = {"seq": z * ROW + lax.rem(y + 2, ROW)}

    barrier = pltpu.get_barrier_semaphore()
    for d in range(1, n_tp):
        pl.semaphore_signal(barrier, inc=1, device_id={"tp": lax.rem(t + d, n_tp)}, device_id_type=MESH)
    near = [z * ROW + lax.rem(y + d, ROW) for d in (1, 2, 3)]
    near += [lax.rem(z + d, rows) * ROW + y for d in (1, 2, 3)]
    for n in near:
        pl.semaphore_signal(barrier, inc=1, device_id={"seq": n}, device_id_type=MESH)

    own = 8 + y
    loads = [
        pltpu.make_async_copy(k_in, kbuf.at[own, 0:tokens], in_sem.at[0]),
        pltpu.make_async_copy(v_in, vbuf.at[own], in_sem.at[1]),
        pltpu.make_async_copy(q_in, q, in_sem.at[2]),
        pltpu.make_async_copy(do_in, do, in_sem.at[3]),
    ]
    for c in loads:
        c.start()
    docf = doc[...].astype(F32)
    kbuf[own, tokens : tokens + PAD, :] = jnp.concatenate(
        [docf[:, 0:HEAD], docf[:, HEAD:], jnp.zeros((PAD - 2, HEAD), F32)], axis=0
    ).astype(BF16)
    for r in range(2):

        @pl.when(z + r < 2)
        def _():
            for i in range(ROW):
                kbuf[r * ROW + i, 0:tokens, :] = jnp.zeros((tokens, HEAD), BF16)
                kbuf[r * ROW + i, tokens : tokens + PAD, :] = jnp.full((PAD, HEAD), -1.0, BF16)
                vbuf[r * ROW + i, :, :] = jnp.zeros((tokens, HEAD), BF16)

    for c in loads:
        c.wait()
    pl.semaphore_wait(barrier, n_tp - 1 + len(near))

    started = []

    def send(when, src, dst, ssem, rsem, to):
        def make():
            return pltpu.make_async_remote_copy(src(), dst(), ssem(), rsem(), device_id=to, device_id_type=MESH)

        @pl.when(when())
        def _():
            make().start()

        started.append((when, make))

    def send_block(when, slot, dst_slot, half, index, to):
        buf = (kbuf, vbuf)[half]
        send(
            when, lambda: buf.at[slot], lambda: buf.at[dst_slot],
            lambda: kv_send.at[index], lambda: kv_recv.at[2 * dst_slot + half], to,
        )

    def wait_block(when, slot, halves=(0, 1)):
        for half in halves:
            buf = (kbuf, vbuf)[half]

            @pl.when(when)
            def _():
                pltpu.make_async_remote_copy(
                    buf.at[slot], buf.at[slot], kv_send.at[0], kv_recv.at[2 * slot + half],
                    device_id=right, device_id_type=MESH,
                ).wait_recv()

    has1, has2 = z >= 1, z >= 2
    for half in range(2):
        send_block(lambda: z + 1 < rows, own, 4 + y, half, half, {"seq": lax.rem(s + ROW, n_seq)})
    for half in range(2):
        send_block(lambda: y <= 2, own, own, half, 2 + half, right)
        send_block(lambda: y == 0, own, own, half, 4 + half, left)
        send_block(lambda: y <= 1, own, own, half, 6 + half, opposite)
    for half in range(2):
        send_block(lambda: z + 2 < rows, own, y, half, 8 + half, below)
    for half in range(2):
        send(
            lambda: (z + 2 < rows) & (y >= 2),
            lambda half=half: (kbuf, vbuf)[half].at[own],
            lambda half=half: (kvia, vvia)[half],
            lambda half=half: via_send.at[half],
            lambda half=half: via_recv.at[half],
            opposite,
        )
    do_copies = []
    for d in (2, 6, 4, 3, 5, 7, 1):
        p = lax.rem(t + d, n_tp)
        c = pltpu.make_async_remote_copy(
            do.at[:, pl.ds(pl.multiple_of(p * cols, cols), cols)],
            dog.at[pl.ds(pl.multiple_of(t * rows_do, rows_do), rows_do), :],
            do_send.at[d - 1],
            do_recv.at[d - 1],
            device_id={"tp": p},
            device_id_type=MESH,
        )
        c.start()
        do_copies.append(c)
    dog[pl.ds(pl.multiple_of(t * rows_do, rows_do), rows_do), :] = do[
        :, pl.ds(pl.multiple_of(t * cols, cols), cols)
    ]

    col1, own_left, y1, y2 = 4 + y, own - 1, y + 1, y + 2
    slots_a = [jnp.where(y + e < ROW, y + e, y + e + 4) for e in range(4)]
    slots_b = [4 + lax.rem(y + e, ROW) for e in range(4)]
    to1 = {"seq": lax.rem(s + n_seq - ROW, n_seq)}
    to2 = {"seq": lax.rem(s + n_seq - 2 * ROW, n_seq)}

    def slot_a(e):
        return slots_a[e]

    def slot_b(e):
        return slots_b[e]

    key_at = lax.broadcasted_iota(jnp.int32, (tokens, tokens), 0)
    query_at = lax.broadcasted_iota(jnp.int32, (tokens, tokens), 1)

    def head_rows(h):
        return pl.ds(pl.multiple_of(h * tokens, tokens), tokens)

    for h in range(heads):
        scaled = q[:, h * HEAD : (h + 1) * HEAD].astype(F32) * FACTOR2
        high = scaled.astype(BF16)
        qs[h * tokens : (h + 1) * tokens, 0:HEAD] = high
        qs[h * tokens : (h + 1) * tokens, HEAD:] = (scaled - high.astype(F32)).astype(BF16)

    def scores(slot, diagonal):
        w = slot - y
        kb = jnp.concatenate([kbuf[slot, 0:tokens, :]] * 2, axis=1)
        docs = kbuf[slot, tokens : tokens + PAD, :].astype(F32)[0:2, :]
        low = jnp.zeros((1, tokens), F32)
        for d in range(DOCS):
            count = jnp.sum(jnp.where(docs < d, 1.0, 0.0), axis=(0, 1), keepdims=True)
            low = low + jnp.where(docf == d, count, 0.0)
        seen = key_at >= low.astype(jnp.int32)
        if diagonal:
            seen = seen & (key_at <= query_at)
        bias[...] = jnp.where(seen, 0.0, BIG)

        def one(h, c):
            sc = dot_nt(kb, qs[head_rows(h), :]) + bias[...]
            top = jnp.max(sc, axis=0, keepdims=True)
            if not diagonal:
                old = peak[h]
                top = jnp.maximum(old, top)
            e = jnp.exp2(sc - top)
            part = jnp.sum(e, axis=0, keepdims=True)
            if not diagonal:
                part = part + total[h] * jnp.exp2(old - top)
            total[h] = part
            peak[h] = top
            peak_blk[w, h] = top
            e_ref[w, h] = e
            return c

        lax.fori_loop(0, heads, one, 0, unroll=heads)

    def here(slot):
        return jnp.where(slot >= 8, True, jnp.where(slot >= 4, has1, has2))

    def weight_grads(slot):
        w = slot - y
        known = (slot == own) | (slot == 4 + y) | (slot == y) | (slot == slot_b(1))
        wait_block(here(slot) & jnp.logical_not(known), slot, (1,))
        vb = vbuf[slot]

        def one(h, c):
            dp = dot_nt(vb, gs[head_rows(h), :])
            p_ref[w, h] = dp
            w_blk[w, h] = jnp.sum(e_ref[w, h] * dp, axis=0, keepdims=True)
            return c

        lax.fori_loop(0, heads, one, 0, unroll=heads)

    scores(own, True)
    for h in range(heads):
        qt[:, h * tokens : (h + 1) * tokens] = q[:, h * HEAD : (h + 1) * HEAD].T

    def first_stage():
        for half in range(2):
            wait_block(has1, 4 + y, (half,))
            send_block(lambda: has1, col1, col1, half, 12 + half, right)
            send_block(lambda: has1, col1, col1, half, 14 + half, left)

    def step_slot(k):
        late = k - 6 - y
        return pick(
            k,
            [
                own,
                4 + y,
                *[
                    jnp.where(
                        k < 2 + y,
                        pick(y, [8, 8, jnp.where(k == 2, 9, 8), jnp.where(k == 2, 10, jnp.where(k == 3, 8, 9))]),
                        jnp.where(
                            k < 6 + y,
                            pick(k - 2 - y, [y, slot_b(3), slot_b(1), slot_b(2)]),
                            pick(y, [pick(late, [1, 3, 2]), pick(late, [2, 3]), 3, 3]),
                        ),
                    )
                ]
                * 7,
            ],
        )

    first_stage()

    def gather_do():
        for c in do_copies:
            c.wait_recv()
        for h in range(heads):
            gs[h * tokens : (h + 1) * tokens, :] = dog[:, h * HEAD : (h + 1) * HEAD]
            gt[:, h * tokens : (h + 1) * tokens] = dog[:, h * HEAD : (h + 1) * HEAD].T

    def loop(k, c):
        @pl.when(k == jnp.minimum(2 + y, 3))
        def _():
            for half in range(2):
                via = (kvia, vvia)[half]

                @pl.when((z + 2 < rows) & (y <= 1))
                def _():
                    pltpu.make_async_remote_copy(
                        via, via, via_send.at[half], via_recv.at[half], device_id=right, device_id_type=MESH
                    ).wait_recv()

                send(
                    lambda: (z + 2 < rows) & (y <= 1),
                    lambda half=half: (kvia, vvia)[half],
                    lambda half=half: (kbuf, vbuf)[half].at[y2],
                    lambda half=half: kv_send.at[10 + half],
                    lambda half=half: kv_recv.at[2 * y2 + half],
                    below,
                )

            for half in range(2):
                wait_block(has2, y, (half,))
                send_block(lambda: has2 & (y == 3), y, y, half, 16 + half, right)
                send_block(lambda: has2 & (y >= 1), y, y, half, 18 + half, left)

        @pl.when(k == jnp.minimum(3 + y, 4))
        def _():
            wait_block(has1, slot_b(3), (0,))
            send_block(lambda: has1, slot_b(3), slot_b(3), 0, 20, right)
            wait_block(has1, slot_b(1), (1,))
            send_block(lambda: has1, slot_b(1), slot_b(1), 1, 21, left)

        @pl.when(k == 5 + y)
        def _():
            gather_do()

            def early(j, c):
                weight_grads(step_slot(j))
                return c

            lax.fori_loop(0, 5 + y, early, 0)

        @pl.when(k > 5 + y)
        def _():
            weight_grads(step_slot(k - 1))

        slot = step_slot(k)
        known = (slot == own) | (slot == 4 + y) | (slot == y) | (slot == slot_b(3))
        wait_block(here(slot) & jnp.logical_not(known), slot, (0,))
        scores(slot, False)
        return c

    lax.fori_loop(1, 9, loop, 0)

    weight_grads(step_slot(jnp.int32(8)))

    def stats(h, c):
        inv = 1.0 / total[h]
        acc = jnp.zeros((1, tokens), F32)
        for w in range(9):
            f = jnp.exp2(peak_blk[w, h] - peak[h]) * inv
            f_ref[w, h] = f
            acc = acc + f * w_blk[w, h]
        row_dot[h] = acc
        return c

    lax.fori_loop(0, heads, stats, 0)

    order = [slot_b(2), slot_a(2), slot_b(1), slot_b(3), slot_a(1), slot_a(3), y, 4 + y, own]
    halves = (pk, pv)

    def rs(when, src, dst, index, to):
        send(when, src, dst, lambda: rs_send.at[index], lambda: rs_recv.at[index], to)

    def rs_wait(when, dst, index):
        @pl.when(when)
        def _():
            pltpu.make_async_remote_copy(
                dst, dst, rs_send.at[index], rs_recv.at[index], device_id=right, device_id_type=MESH
            ).wait_recv()

    def add(when, half, slot, other):
        @pl.when(when)
        def _():
            halves[half][slot] = (halves[half][slot].astype(F32) + other[...].astype(F32)).astype(BF16)

    a2_any = has2 | (y >= 2)
    a1_any = has2 | (y == 3)
    a3_any = has2 | (y >= 1)

    def after(j):
        if j == 0:
            rs(lambda: has1, lambda: pk.at[slot_b(2)], lambda: rel.at[0], 0, right)
            rs(lambda: has1, lambda: pv.at[slot_b(2)], lambda: rel.at[1], 1, left)
        if j == 1:
            sl = slot_a(2)
            rs(lambda: has2 & (y == 0), lambda: pk.at[sl], lambda: rel.at[2], 2, right)
            rs(lambda: a2_any & (y >= 1), lambda: pk.at[sl], lambda: rel.at[3], 3, left)
            rs(lambda: a2_any & (y <= 2), lambda: pv.at[sl], lambda: rel.at[4], 4, right)
            rs(lambda: y == 3, lambda: pv.at[sl], lambda: rel.at[5], 5, left)
        if j == 2:
            rs(lambda: has1, lambda: pv.at[slot_b(1)], lambda: msg_b.at[1], 7, right)
        if j == 3:
            rs(lambda: has1, lambda: pk.at[slot_b(3)], lambda: msg_b.at[2], 8, left)
            rs_wait(has1, rel.at[0], 0)
            add(has1, 0, slot_b(1), rel.at[0])
            rs(lambda: has1, lambda: pk.at[slot_b(1)], lambda: msg_b.at[0], 6, right)
            rs_wait(has1, rel.at[1], 1)
            add(has1, 1, slot_b(3), rel.at[1])
            rs(lambda: has1, lambda: pv.at[slot_b(3)], lambda: msg_b.at[3], 9, left)
        if j == 4:
            sl = slot_a(1)
            rs_wait(has2 & (y == 1), rel.at[2], 2)
            add(has2 & (y == 1), 0, sl, rel.at[2])
            rs(lambda: a1_any, lambda: pk.at[sl], lambda: msg_a.at[0], 10, right)
            got_v = (has2 & (y >= 1)) | (y == 3)
            rs_wait(got_v, rel.at[4], 4)
            add(got_v, 1, sl, rel.at[4])
            rs(lambda: a1_any, lambda: pv.at[sl], lambda: msg_a.at[1], 11, right)
        if j == 5:
            sl = slot_a(3)
            got_k = (has2 & (y == 0)) | (y == 1) | (y == 2)
            rs_wait(got_k, rel.at[3], 3)
            add(got_k, 0, sl, rel.at[3])
            rs(lambda: a3_any, lambda: pk.at[sl], lambda: msg_a.at[2], 12, left)
            rs_wait(y == 2, rel.at[5], 5)
            add(y == 2, 1, sl, rel.at[5])
            rs(lambda: a3_any, lambda: pv.at[sl], lambda: msg_a.at[3], 13, left)
        if j == 7:
            for half in range(2):
                rs_wait(has1, msg_b.at[half], 6 + half)
                add(has1, half, 4 + y, msg_b.at[half])
                rs_wait(has1, msg_b.at[2 + half], 8 + half)
                add(has1, half, 4 + y, msg_b.at[2 + half])
                rs(lambda: has1, lambda half=half: halves[half].at[col1], lambda half=half: down.at[half], 14 + half, to1)
            from_left = (has2 & (y >= 1)) | (y == 0)
            from_right = (has2 & (y == 3)) | (y <= 2)
            for half in range(2):
                rs_wait(from_left, msg_a.at[half], 10 + half)
                rs_wait(from_right, msg_a.at[2 + half], 12 + half)
                add(has2 & (y >= 1), half, y, msg_a.at[half])
                add(has2 & (y == 3), half, y, msg_a.at[2 + half])
                rs(lambda: has2, lambda half=half: halves[half].at[y], lambda half=half: down.at[2 + half], 16 + half, to2)

    def block_grads(j):
        slot = pick(j, order)
        w = slot - y
        dvt = jnp.zeros((HEAD, tokens), F32)
        dkt = jnp.zeros((HEAD, tokens), F32)
        for h in range(heads):
            hs = slice(h * tokens, (h + 1) * tokens)
            p = e_ref[w, h] * f_ref[w, h]
            ds = (p * (p_ref[w, h] - row_dot[h])).astype(BF16)
            ds_ref[w, h] = ds
            dvt = dvt + dot_nt(gt[:, hs], p.astype(BF16))
            dkt = dkt + dot_nt(qt[:, hs], ds)
        dkt = dkt * FACTOR
        pk[slot] = dkt.astype(BF16)
        pv[slot] = dvt.astype(BF16)

        @pl.when(j == 8)
        def _():
            dkv[0] = dkt
            dkv[1] = dvt

    def grads(j, c):
        block_grads(j)
        for i in range(8):

            @pl.when(j == i)
            def _():
                after(i)

        return c

    lax.fori_loop(0, 9, grads, 0)

    for w in range(9):
        keysT[:, w * tokens : (w + 1) * tokens] = kbuf[y + w, 0:tokens, :].astype(F32).T.astype(BF16)

    def query(h, c):
        acc = jnp.zeros((HEAD, tokens), F32)
        for w in range(9):
            acc = acc + dot_nn(keysT[:, w * tokens : (w + 1) * tokens], ds_ref[w, h])
        dq_out[:, pl.ds(pl.multiple_of(h * HEAD, HEAD), HEAD)] = (acc.T * FACTOR).astype(BF16)
        return c

    lax.fori_loop(0, heads, query, 0)

    for half in range(2):

        @pl.when(y == 0)
        def _():
            dkv[half] += msg_a[half].astype(F32)

        @pl.when(y <= 2)
        def _():
            dkv[half] += msg_a[2 + half].astype(F32)

    for i, when in ((0, z + 1 < rows), (2, z + 2 < rows)):
        for half in range(2):
            rs_wait(when, down.at[i + half], 14 + i + half)

            @pl.when(when)
            def _():
                dkv[half] += down[i + half].astype(F32)

    dk_out[...] = dkv[0].T.astype(BF16)
    dv_out[...] = dkv[1].T.astype(BF16)
    for c in do_copies:
        c.wait_send()
    for when, make in started:

        @pl.when(when())
        def _():
            make().wait_send()


def write_out(a, b, c, a_out, b_out, c_out, sem):
    copies = [
        pltpu.make_async_copy(src, dst, sem.at[i])
        for i, (src, dst) in enumerate(((a, a_out), (b, b_out), (c, c_out)))
    ]
    for copy in copies:
        copy.start()
    for copy in copies:
        copy.wait()


def solution(mesh):
    n_seq, n_tp = mesh.shape["seq"], mesh.shape["tp"]

    def local(queries, key_matrix, value_matrix, output_gradient, document):
        tokens, cols = queries.shape
        heads = cols // HEAD
        hbm = pl.BlockSpec(memory_space=pltpu.HBM)
        vm = pl.BlockSpec(memory_space=pltpu.VMEM)
        dma = pltpu.SemaphoreType.DMA
        v = pltpu.VMEM
        grads = pl.pallas_call(
            functools.partial(kernel, n_seq, n_tp),
            out_shape=[
                jax.ShapeDtypeStruct((tokens, cols), BF16),
                jax.ShapeDtypeStruct((tokens, HEAD), BF16),
                jax.ShapeDtypeStruct((tokens, HEAD), BF16),
            ],
            in_specs=[hbm] * 4 + [vm],
            out_specs=[vm] * 3,
            scratch_shapes=[
                v((tokens, cols), BF16),
                v(output_gradient.shape, BF16),
                v((tokens, cols), BF16),
                v((12, tokens + PAD, HEAD), BF16),
                v((12, tokens, HEAD), BF16),
                v((heads * tokens, 2 * HEAD), BF16),
                v((heads * tokens, HEAD), BF16),
                v((HEAD, 9 * tokens), BF16),
                v((9, heads, tokens, tokens), F32),
                v((9, heads, tokens, tokens), F32),
                v((9, heads, tokens, tokens), BF16),
                v((tokens, tokens), F32),
                v((HEAD, heads * tokens), BF16),
                v((HEAD, heads * tokens), BF16),
                v((9, heads, 1, tokens), F32),
                v((9, heads, 1, tokens), F32),
                v((9, heads, 1, tokens), F32),
                v((heads, 1, tokens), F32),
                v((heads, 1, tokens), F32),
                v((heads, 1, tokens), F32),
                v((12, HEAD, tokens), BF16),
                v((12, HEAD, tokens), BF16),
                v((6, HEAD, tokens), BF16),
                v((4, HEAD, tokens), BF16),
                v((4, HEAD, tokens), BF16),
                v((4, HEAD, tokens), BF16),
                v((2, HEAD, tokens), F32),
                v((tokens + PAD, HEAD), BF16), v((tokens, HEAD), BF16), dma((2,)), dma((2,)),
                dma((4,)), dma((n_tp - 1,)), dma((n_tp - 1,)),
                dma((24,)), dma((24,)), dma((18,)), dma((18,)),
            ],
            compiler_params=pltpu.CompilerParams(
                collective_id=0, has_side_effects=True, vmem_limit_bytes=63 * 1024 * 1024
            ),
        )(queries, key_matrix, value_matrix, output_gradient, document.reshape(1, tokens))
        return pl.pallas_call(
            write_out,
            out_shape=[jax.ShapeDtypeStruct(g.shape, g.dtype) for g in grads],
            in_specs=[vm] * 3,
            out_specs=[hbm] * 3,
            scratch_shapes=[dma((3,))],
        )(*grads)

    return jax.shard_map(
        local,
        mesh=mesh,
        in_specs=(P("seq", "tp"), P("seq", "tp"), P("seq", "tp"), P(("seq", "tp"), None), P("seq")),
        out_specs=(P("seq", "tp"),) * 3,
        check_vma=False,
    )
```
